256 devices in a mesh: seq: 32 (over x, z_lo, core), head: 8 (over z_hi, y).
Axes of the slice: x: 4, y: 4, z: 8 (z_hi: 2, z_lo: 4; z = z_hi * 4 + z_lo), core: 2. Of those that a mesh axis runs over, the one named last changes fastest.
Arguments:
- queries: bfloat16 [8192, 8192], P('seq', 'head'), may hold values from -4.6 to 4.6
- keys: bfloat16 [8192, 1024], P('seq', 'head'), may hold values from -4.6 to 4.6
- values: bfloat16 [8192, 1024], P('seq', 'head'), may hold values from -4 to 4
- key_keep: int32 [8192], P('seq'), may hold values 0 or 1
- global_positions: int32 [384], replicated, may hold values from 0 to 8191
- gain: bfloat16 [8192], P('head'), may hold values from 0.5 to 1.5
- cotangent: bfloat16 [8192, 8192], P('seq', 'head'), may hold values from -6 to 6
Outputs:
- normed: bfloat16 [8192, 8192], P('seq', 'head')
- query_grad: bfloat16 [8192, 8192], P('seq', 'head')
- key_grad: bfloat16 [8192, 1024], P('seq', 'head')
- value_grad: bfloat16 [8192, 1024], P('seq', 'head')
The draws below stay inside these ranges and needn't reach their ends.
All inputs are finite; a program needn't handle non-finite values. No bound on the sum of `key_keep` on one device may be relied on, other than what follows from the above.
Results may differ from the reference program's by a relative error of at most 0.018.
Values may be sent and summed in bfloat16 or wider, within the bound.
A program may use at most 64 MiB of HBM per device.

```python
import jax
import jax.numpy as jnp
from jax import lax

QH = 64
KVH = 8
HD = 128
S_DEV = 256
GLOBALS = 384
TOKENS = 8192
LEVELS = 5
N_SEQ = 32


def shared_keys(key):
    entries = jnp.clip(jax.random.normal(jax.random.fold_in(key, 11), (TOKENS, KVH * HD), jnp.float32), -4.0, 4.0)
    return entries


def draw_keys(key, part):
    entries = shared_keys(key)
    return entries.astype(jnp.bfloat16)


def draw_queries(key, part):
    drawn_queries = jnp.clip(jax.random.normal(jax.random.fold_in(key, 21), (TOKENS, QH * HD), jnp.float32), -4.0, 4.0)
    return drawn_queries.astype(jnp.bfloat16)


def draw_values(key, part):
    drawn = jax.random.normal(jax.random.fold_in(key, 31), (TOKENS, KVH * HD), jnp.float32)
    return jnp.clip(drawn, -4.0, 4.0).astype(jnp.bfloat16)


def draw_cotangent(key, part):
    query_all = draw_queries(key, part).astype(jnp.float32)
    key_all = draw_keys(key, part).astype(jnp.float32)
    value_all = draw_values(key, part).astype(jnp.float32)
    shard_count = TOKENS // S_DEV
    group_size = QH // KVH
    key_shards = key_all.reshape(shard_count, S_DEV, KVH * HD)
    value_shards = value_all.reshape(shard_count, S_DEV, KVH * HD)

    def shard_mix(shard_index):
        partners = [shard_index] + [jnp.bitwise_xor(shard_index, 1 << level_bit) for level_bit in range(LEVELS)]
        chosen_ids = jnp.stack(partners).astype(jnp.int32)
        near_keys = key_shards[chosen_ids].reshape(-1, KVH, HD)
        near_values = value_shards[chosen_ids].reshape(-1, KVH, HD)
        start_row = (shard_index * S_DEV).astype(jnp.int32)
        own_queries = lax.dynamic_slice_in_dim(query_all, start_row, S_DEV, 0).reshape(S_DEV, KVH, group_size, HD)
        scores = jnp.einsum('sagd,kad->agsk', own_queries, near_keys) * HD ** (-0.5)
        weights = jax.nn.softmax(scores, -1)
        mixed = jnp.einsum('agsk,kad->sagd', weights, near_values)
        return mixed.reshape(S_DEV, QH * HD)
    attn_guess = lax.map(shard_mix, jnp.arange(shard_count, dtype=jnp.int32)).reshape(TOKENS, QH * HD)
    direction = attn_guess * lax.rsqrt(jnp.mean(attn_guess * attn_guess, -1, keepdims=True) + 1e-06)
    noise = jnp.clip(jax.random.normal(jax.random.fold_in(key, 41), (TOKENS, QH * HD), jnp.float32), -4.0, 4.0)
    strength = jax.random.uniform(jax.random.fold_in(key, 42), (TOKENS, 1), jnp.float32, 0.5, 1.5)
    return jnp.clip(noise + strength * direction, -6.0, 6.0).astype(jnp.bfloat16)


def set_ends(values, key, smallest, top_value):
    shape = values.shape
    index_at = [jax.random.randint(jax.random.fold_in(key, axis), (), 0, shape[axis]) for axis in range(len(shape))]
    values = values.at[tuple(index_at)].set(smallest)
    longest = shape.index(max(shape))
    index_at[longest] = (index_at[longest] + 1) % shape[longest]
    return values.at[tuple(index_at)].set(top_value)


def setup_inputs(seed: int = 0) -> dict:
    splits = jax.random.split(jax.random.key(seed), 8)
    queries = draw_queries(jax.random.fold_in(splits[7], 71), 0)
    keys = draw_keys(jax.random.fold_in(splits[7], 71), 0)
    values = draw_values(jax.random.fold_in(splits[7], 71), 0)
    key_keep = set_ends((jax.random.randint(splits[3], (TOKENS,), 0, 8) < 7).astype(jnp.int32), jax.random.fold_in(splits[3], 1), 0, 1)
    global_positions = set_ends(jax.random.randint(splits[4], (GLOBALS,), 0, TOKENS), jax.random.fold_in(splits[4], 1), 0, TOKENS - 1).astype(jnp.int32)
    gain = jnp.clip(1.0 + 0.1 * jax.random.normal(splits[5], (QH * HD,), jnp.float32), 0.5, 1.5).astype(jnp.bfloat16)
    cotangent = draw_cotangent(jax.random.fold_in(splits[7], 71), 0)
    return dict(queries=queries, keys=keys, values=values, key_keep=key_keep, global_positions=global_positions, gain=gain, cotangent=cotangent)


NEG_FILL = -1e+30
NORM_EPS = 1e-06

def shard_terms(shard_index, queries, keys, values, key_keep, global_positions, gain, cotangent):
    feature_width = KVH * HD
    group_size = QH // KVH
    scaling = HD ** (-0.5)
    offset_rows = (shard_index * S_DEV).astype(jnp.int32)
    own_queries = lax.dynamic_slice_in_dim(queries, offset_rows, S_DEV, 0)
    own_cotangent = lax.dynamic_slice_in_dim(cotangent, offset_rows, S_DEV, 0)
    own_keep = lax.dynamic_slice_in_dim(key_keep, offset_rows, S_DEV, 0)
    key_blocks = [lax.dynamic_slice_in_dim(keys, offset_rows, S_DEV, 0)]
    value_blocks = [lax.dynamic_slice_in_dim(values, offset_rows, S_DEV, 0)]
    masks = [(own_keep[None, :] == 1) | jnp.eye(S_DEV, dtype=bool)]
    for level_bit in range(LEVELS):
        partner_rows = (jnp.bitwise_xor(shard_index, 1 << level_bit) * S_DEV).astype(jnp.int32)
        key_blocks.append(lax.dynamic_slice_in_dim(keys, partner_rows, S_DEV, 0))
        value_blocks.append(lax.dynamic_slice_in_dim(values, partner_rows, S_DEV, 0))
        partner_keep = lax.dynamic_slice_in_dim(key_keep, partner_rows, S_DEV, 0)
        masks.append(jnp.broadcast_to(partner_keep[None, :] == 1, (S_DEV, S_DEV)))
    key_blocks.append(keys[global_positions])
    value_blocks.append(values[global_positions])
    masks.append(jnp.broadcast_to(key_keep[global_positions][None, :] == 1, (S_DEV, GLOBALS)))
    all_keys = jnp.concatenate(key_blocks, 0)
    all_values = jnp.concatenate(value_blocks, 0)
    visible = jnp.concatenate(masks, 1)
    slots = all_keys.shape[0]
    query_heads = own_queries.reshape(S_DEV, KVH, group_size, HD).astype(jnp.float32)
    key_heads = all_keys.reshape(slots, KVH, HD).astype(jnp.float32)
    value_heads = all_values.reshape(slots, KVH, HD).astype(jnp.float32)
    scores = jnp.einsum('sagd,kad->agsk', query_heads, key_heads) * scaling
    scores = jnp.where(visible[None, None], scores, NEG_FILL)
    peak = lax.optimization_barrier(jnp.max(scores, -1, keepdims=True))
    expo = jnp.exp(scores - peak)
    total = lax.optimization_barrier(jnp.sum(expo, -1, keepdims=True))
    expo_bf = expo.astype(jnp.bfloat16).astype(jnp.float32)
    mixed = jnp.einsum('agsk,kad->agsd', expo_bf, value_heads) / total
    attn = jnp.transpose(mixed, (2, 0, 1, 3)).reshape(S_DEV, QH * HD)
    feature_count = QH * HD
    squares = lax.optimization_barrier(jnp.sum(attn * attn, -1))
    inverse = lax.rsqrt(squares / feature_count + NORM_EPS)
    gain_wide = gain.astype(jnp.float32)
    normed = (attn * inverse[:, None] * gain_wide).astype(jnp.bfloat16)
    upstream = own_cotangent.astype(jnp.float32) * gain_wide
    crossed = lax.optimization_barrier(jnp.sum(upstream * attn, -1))
    d_attn = inverse[:, None] * upstream - attn * (inverse ** 3 * crossed / feature_count)[:, None]
    d_attn_bf = d_attn.astype(jnp.bfloat16).astype(jnp.float32)
    d_heads = d_attn.reshape(S_DEV, KVH, group_size, HD)
    d_heads_bf = d_attn_bf.reshape(S_DEV, KVH, group_size, HD)
    attn_heads = attn.reshape(S_DEV, KVH, group_size, HD)
    probs = expo / total
    d_probs = jnp.einsum('sagd,kad->agsk', d_heads_bf, value_heads)
    diag_term = jnp.einsum('sagd,sagd->ags', d_heads, attn_heads)[..., None]
    d_scores = (probs * (d_probs - diag_term)).astype(jnp.bfloat16).astype(jnp.float32)
    probs_bf = probs.astype(jnp.bfloat16).astype(jnp.float32)
    d_query = jnp.einsum('agsk,kad->sagd', d_scores, key_heads) * scaling
    d_query = d_query.reshape(S_DEV, QH * HD).astype(jnp.bfloat16)
    d_key = (jnp.einsum('agsk,sagd->kad', d_scores, query_heads) * scaling).reshape(slots, feature_width)
    d_value = jnp.einsum('agsk,sagd->kad', probs_bf, d_heads_bf).reshape(slots, feature_width)
    return (normed, d_query, d_key, d_value)

def spread_back(slot_grads, global_positions):
    running = slot_grads[:, :S_DEV]
    shard_ids = jnp.arange(N_SEQ, dtype=jnp.int32)
    for level_bit in range(LEVELS):
        block = slot_grads[:, S_DEV * (level_bit + 1):S_DEV * (level_bit + 2)]
        running = running + block[jnp.bitwise_xor(shard_ids, 1 << level_bit)]
    global_sum = lax.optimization_barrier(jnp.sum(slot_grads[:, S_DEV * (LEVELS + 1):], 0))
    running = running.reshape(TOKENS, KVH * HD).at[global_positions].add(global_sum)
    return running.astype(jnp.bfloat16)

def reference(queries, keys, values, key_keep, global_positions, gain, cotangent):

    def per_shard(shard_index):
        return shard_terms(shard_index, queries, keys, values, key_keep, global_positions, gain, cotangent)
    normed, query_grad, key_slots, value_slots = lax.map(per_shard, jnp.arange(N_SEQ, dtype=jnp.int32))
    normed = normed.reshape(TOKENS, QH * HD)
    query_grad = query_grad.reshape(TOKENS, QH * HD)
    key_grad = spread_back(key_slots, global_positions)
    value_grad = spread_back(value_slots, global_positions)
    return (normed, query_grad, key_grad, value_grad)
```

```python
import functools

import jax
import jax.numpy as jnp
from jax import lax
from jax.experimental import pallas as pl
from jax.experimental.pallas import tpu as pltpu
from jax.sharding import Mesh
from jax.sharding import PartitionSpec as P

HD = 128
FEATURES = 8192
NEG_FILL = -1e30
NORM_EPS = 1e-06
SEQ = ("x", "z", "c")
HEAD = ("zh", "y")
SCALE = HD ** (-0.5)
SCALE2 = SCALE * 1.4426950408889634
F32 = jnp.float32
BF = jnp.bfloat16
H = 8
R = 256
G = 384
SLOTS = 6 * R + G

BLOCKS = [(R * i, R) for i in range(6)] + [(6 * R, G)]
GROUPS = [(0,), (1, 2), (4, 3), (5,), (6,)]


def nt(a, b):
    return lax.dot_general(a, b, (((1,), (1,)), ((), ())), preferred_element_type=F32)


def nn(a, b):
    return jnp.dot(a, b, preferred_element_type=F32)


def tn(a, b):
    return lax.dot_general(a, b, (((0,), (0,)), ((), ())), preferred_element_type=F32)


def wide(x, n):
    return jnp.concatenate([x] * (n // 128), 1)


def head_cols(h):
    return pl.ds(pl.multiple_of(h * HD, HD), HD)


def kernel(
    q_ref, k_ref, v_ref, keep_ref, gpos_ref, gain_ref, ct_ref,
    normed_ref, dq_ref, dk_ref, dv_ref,
    ks, vs, keeps, own_bias, expo, m_s, l_s, o_s, f_s, attn, d_attn, diag, dqs, dks, dvs,
    ga, gc, hb, gx, pb, gz, hfull, full,
    fl, flc, flx, flz,
    st, st_in, grad_out, grad_in,
    kv_send, kv_recv, g_send, g_recv, f_send, f_recv, st_send, st_recv, gr_send, gr_recv,
):
    x, z, c = lax.axis_index("x"), lax.axis_index("z"), lax.axis_index("c")
    zh, y = lax.axis_index("zh"), lax.axis_index("y")
    x_peers = [lax.rem(x + o, 4) for o in (1, 2, 3)]
    z_peers = [lax.rem(z + o, 4) for o in (1, 2, 3)]
    head_peers = [
        {"zh": lax.rem(zh + dz, 2), "y": lax.rem(y + dy, 4)}
        for dz in range(2)
        for dy in range(4)
        if dz or dy
    ]
    partners = [
        {"c": 1 - c},
        {"z": z + 1 - 2 * lax.rem(z, 2)},
        {"z": lax.rem(z + 2, 4)},
        {"x": x + 1 - 2 * lax.rem(x, 2)},
        {"x": lax.rem(x + 2, 4)},
    ]

    def remote(src, dst, send, recv, device):
        return pltpu.make_async_remote_copy(
            src_ref=src, dst_ref=dst, send_sem=send, recv_sem=recv,
            device_id=device, device_id_type=pl.DeviceIdType.MESH,
        )

    barrier = pltpu.get_barrier_semaphore()
    everyone = [{"c": 1 - c}] + [{"x": p} for p in x_peers] + [{"z": p} for p in z_peers] + head_peers
    for peer in everyone:
        pl.semaphore_signal(barrier, inc=1, device_id=peer, device_id_type=pl.DeviceIdType.MESH)

    offset = (x * 8 + z * 2 + c) * R
    rows = lax.broadcasted_iota(jnp.int32, (R, G), 0)
    chosen = (jnp.broadcast_to(gpos_ref[...], (R, G)) - offset == rows).astype(F32).astype(BF)
    own_kv = jnp.concatenate([k_ref[...], v_ref[...]], 1)
    ga[0] = tn(chosen, own_kv).astype(BF).reshape(2, G // 2, 2 * HD)
    keep_rows = jnp.broadcast_to(keep_ref[...], (8, R)).astype(F32).astype(BF)
    fl[0] = nn(keep_rows, chosen)
    eye = lax.broadcasted_iota(jnp.int32, (R, R), 0) == lax.broadcasted_iota(jnp.int32, (R, R), 1)
    row_bias = jnp.where(jnp.broadcast_to(keep_ref[...], (R, R)) == 1, 0.0, NEG_FILL)
    own_bias[...] = jnp.where(eye, 0.0, row_bias)
    ks[0:R] = k_ref[...]
    vs[0:R] = v_ref[...]

    pl.semaphore_wait(barrier, len(everyone))

    def kv_copies(b):
        lower = R * (b + 1)
        return [
            remote(k_ref, ks.at[pl.ds(lower, R)], kv_send.at[0, b], kv_recv.at[0, b], partners[b]),
            remote(v_ref, vs.at[pl.ds(lower, R)], kv_send.at[1, b], kv_recv.at[1, b], partners[b]),
            remote(keep_ref, keeps.at[b], kv_send.at[2, b], kv_recv.at[2, b], partners[b]),
        ]

    def started(copies):
        for copy in copies:
            copy.start()
        return copies

    def waited(copies):
        for copy in copies:
            copy.wait()

    def core_stage(t):
        return remote(ga.at[t, 1 - c], gc.at[t], g_send.at[t, 0], g_recv.at[t, 0], {"c": 1 - c})

    def x_stage(t):
        return [
            remote(hb.at[t, p], gx.at[t, i], g_send.at[t, 1 + i], g_recv.at[t, 1 + i], {"x": p})
            for i, p in enumerate(x_peers)
        ]

    def z_stage(t):
        return [
            remote(pb.at[t], gz.at[t, i], g_send.at[t, 4 + i], g_recv.at[t, 4 + i], {"z": p})
            for i, p in enumerate(z_peers)
        ]

    def x_back(t):
        return [
            remote(hfull.at[t, x], hfull.at[t, x], g_send.at[t, 7 + i], g_recv.at[t, 7 + i], {"x": p})
            for i, p in enumerate(x_peers)
        ]

    def core_back(t):
        return remote(full.at[t, c], full.at[t, c], g_send.at[t, 10], g_recv.at[t, 10], {"c": 1 - c})

    def add_core(t):
        total = ga[t, c].astype(F32) + gc[t].astype(F32)
        hb[t] = total.astype(BF).reshape(4, G // 8, 2 * HD)

    def add_x(t):
        total = hb[t, x].astype(F32)
        for i in range(3):
            total = total + gx[t, i].astype(F32)
        pb[t] = total.astype(BF)

    def add_z(t):
        total = pb[t].astype(F32)
        for i in range(3):
            total = total + gz[t, i].astype(F32)
        hfull[t, x] = total.astype(BF)

    def flag_stage(s):
        if s == 0:
            return [remote(fl.at[0], flc, f_send.at[0], f_recv.at[0], {"c": 1 - c})]
        peers = [{"x": p} for p in x_peers] if s == 1 else [{"z": p} for p in z_peers]
        into = flx if s == 1 else flz
        base = 1 if s == 1 else 4
        return [
            remote(fl.at[s], into.at[i], f_send.at[base + i], f_recv.at[base + i], p)
            for i, p in enumerate(peers)
        ]

    def forward_group(g, bias):
        blocks = [BLOCKS[b] for b in GROUPS[g]]

        def body(h, carry):
            q = q_ref[:, head_cols(h)]
            parts, top = [], None
            for lower, size in blocks:
                s = nt(q, ks[lower : lower + size])
                s = s + (own_bias[...] if lower == 0 else bias[lower])
                parts.append(s)
                for j in range(0, size, 128):
                    piece = s[:, j : j + 128]
                    top = piece if top is None else jnp.maximum(top, piece)
            peak = jnp.broadcast_to(jnp.max(top, 1, keepdims=True), (R, 128)) * SCALE2
            mixed, total = None, None
            for (lower, size), s in zip(blocks, parts):
                e = jnp.exp2(s * SCALE2 - wide(peak, size))
                for j in range(0, size, 128):
                    piece = e[:, j : j + 128]
                    total = piece if total is None else total + piece
                e_bf = e.astype(BF)
                expo[h, :, lower : lower + size] = e_bf
                term = nn(e_bf, vs[lower : lower + size])
                mixed = term if mixed is None else mixed + term
            m_s[g, h] = peak
            l_s[g, h] = jnp.broadcast_to(jnp.sum(total, 1, keepdims=True), (R, 128))
            o_s[g, h] = mixed
            return carry

        lax.fori_loop(0, H, body, 0, unroll=2)

    def backward_group(g, first):
        blocks = [BLOCKS[b] for b in GROUPS[g]]

        def body(h, carry):
            q = q_ref[:, head_cols(h)]
            factor = f_s[g, h]
            grad = (d_attn[h] * factor).astype(BF)
            shift = diag[h] * factor
            q_t, grad_t = q.T, grad.T
            d_query = None
            for lower, size in blocks:
                e = expo[h, :, lower : lower + size]
                d_probs = nt(grad, vs[lower : lower + size])
                d_scores = (e.astype(F32) * (d_probs - wide(shift, size))).astype(BF)
                term = nn(d_scores, ks[lower : lower + size])
                d_query = term if d_query is None else d_query + term
                dks[:, lower : lower + size] += nn(q_t, d_scores)
                dvs[:, lower : lower + size] += nn(grad_t, e)
            if first:
                dqs[h] = d_query
            else:
                dqs[h] += d_query
            return carry

        lax.fori_loop(0, H, body, 0, unroll=2)

    def block_bias(*numbers):
        return {
            BLOCKS[b][0]: jnp.where(keeps[b - 1] == 1, 0.0, NEG_FILL).astype(F32) for b in numbers
        }

    core0 = started([core_stage(0)] + flag_stage(0))
    kv = {b: started(kv_copies(b)) for b in (0, 1)}
    waited(core0)
    add_core(0)
    fl[1] = fl[0] + flc[...]
    x0 = started(x_stage(0) + flag_stage(1))
    kv[3] = started(kv_copies(3))
    kv[4] = started(kv_copies(4))
    forward_group(0, {})
    waited(x0)
    add_x(0)
    fl[2] = fl[1] + flx[0] + flx[1] + flx[2]
    z0 = started(z_stage(0) + flag_stage(2))
    kv[2] = started(kv_copies(2))
    waited(kv[0])
    waited(kv[1])
    forward_group(1, block_bias(1, 2))
    waited(z0)
    add_z(0)
    global_keep = fl[2] + flz[0] + flz[1] + flz[2]
    xb0 = started(x_back(0))
    waited(kv[3])
    waited(kv[2])
    forward_group(2, block_bias(4, 3))
    waited(xb0)
    full[0, c] = hfull[0].reshape(G // 2, 2 * HD)
    cb0 = started([core_back(0)])
    waited(kv[4])
    forward_group(3, block_bias(5))
    waited(cb0)
    for half in range(2):
        lower = 6 * R + half * (G // 2)
        ks[lower : lower + G // 2] = full[0, half, :, :HD]
        vs[lower : lower + G // 2] = full[0, half, :, HD:]
    global_bias = jnp.where(global_keep[0:1] > 0.5, 0.0, NEG_FILL)
    forward_group(4, {6 * R: global_bias})

    def merge(h, carry):
        squares, crossed = carry
        peaks = [m_s[g, h] for g in range(len(GROUPS))]
        peak = functools.reduce(jnp.maximum, peaks)
        weights = [jnp.exp2(p - peak) for p in peaks]
        total = sum(w * l_s[g, h] for g, w in enumerate(weights))
        inv_total = 1.0 / total
        out = None
        for g, w in enumerate(weights):
            factor = w * inv_total
            f_s[g, h] = factor
            term = factor * o_s[g, h]
            out = term if out is None else out + term
        attn[h] = out
        up = ct_ref[:, head_cols(h)].astype(F32) * gain_ref[:, head_cols(h)].astype(F32)
        return (squares + out * out, crossed + up * out)

    zeros = jnp.zeros((R, HD), F32)
    squares, crossed = lax.fori_loop(0, H, merge, (zeros, zeros))
    rows8 = lax.broadcasted_iota(jnp.int32, (8, R), 0)
    squares_row = jnp.broadcast_to(jnp.sum(squares.T, 0, keepdims=True), (8, R))
    crossed_row = jnp.broadcast_to(jnp.sum(crossed.T, 0, keepdims=True), (8, R))
    st[...] = jnp.where(rows8 == 0, squares_row, crossed_row)
    stats = started(
        [
            remote(st, st_in.at[i], st_send.at[i], st_recv.at[i], peer)
            for i, peer in enumerate(head_peers)
        ]
    )
    dks[...] = jnp.zeros_like(dks)
    dvs[...] = jnp.zeros_like(dvs)
    waited(stats)
    both = st[...]
    for i in range(7):
        both = both + st_in[i]
    inverse = lax.rsqrt(both[0:1] / FEATURES + NORM_EPS)
    coef = inverse * inverse * inverse * both[1:2] / FEATURES
    inverse = jnp.broadcast_to(inverse, (HD, R)).T
    coef = jnp.broadcast_to(coef, (HD, R)).T

    def norm_grad(h, carry):
        out = attn[h]
        gain = gain_ref[:, head_cols(h)].astype(F32)
        up = ct_ref[:, head_cols(h)].astype(F32) * gain
        grad = inverse * up - out * coef
        d_attn[h] = grad
        diag[h] = jnp.broadcast_to(jnp.sum(grad * out, 1, keepdims=True), (R, HD))
        normed_ref[:, head_cols(h)] = (out * inverse * gain).astype(BF)
        return carry

    lax.fori_loop(0, H, norm_grad, 0)

    def send_grads(b):
        lower = R * (b + 1)
        grad_out[b, 0] = (dks[:, lower : lower + R] * SCALE).astype(BF)
        grad_out[b, 1] = dvs[:, lower : lower + R].astype(BF)
        return started(
            [remote(grad_out.at[b], grad_in.at[b], gr_send.at[b], gr_recv.at[b], partners[b])]
        )

    backward_group(4, True)
    d_global = jnp.concatenate([dks[:, 6 * R :] * SCALE, dvs[:, 6 * R :]], 0).T
    ga[1] = d_global.astype(BF).reshape(2, G // 2, 2 * HD)
    core1 = started([core_stage(1)])
    backward_group(3, False)
    waited(core1)
    add_core(1)
    x1 = started(x_stage(1))
    sent = send_grads(4)
    backward_group(2, False)
    waited(x1)
    add_x(1)
    z1 = started(z_stage(1))
    sent += send_grads(2) + send_grads(3)
    backward_group(1, False)
    waited(z1)
    add_z(1)
    xb1 = started(x_back(1))
    sent += send_grads(1) + send_grads(0)
    backward_group(0, False)

    def finish(h, carry):
        dq_ref[:, head_cols(h)] = (dqs[h] * SCALE).astype(BF)
        return carry

    lax.fori_loop(0, H, finish, 0)
    waited(xb1)
    full[1, c] = hfull[1].reshape(G // 2, 2 * HD)
    cb1 = started([core_back(1)])
    waited(sent)
    d_keys = dks[:, 0:R] * SCALE
    d_values = dvs[:, 0:R]
    for b in range(5):
        d_keys = d_keys + grad_in[b, 0].astype(F32)
        d_values = d_values + grad_in[b, 1].astype(F32)
    waited(cb1)
    back = nn(chosen, full[1].reshape(G, 2 * HD))
    dk_ref[...] = (d_keys.T + back[:, :HD]).astype(BF)
    dv_ref[...] = (d_values.T + back[:, HD:]).astype(BF)


def per_device(queries, keys, values, key_keep, global_positions, gain, cotangent):
    vmem = pl.BlockSpec(memory_space=pltpu.VMEM)
    ng = len(GROUPS)
    half, eighth, width = G // 2, G // 8, 2 * HD
    scratch = [
        pltpu.VMEM((SLOTS, HD), BF),
        pltpu.VMEM((SLOTS, HD), BF),
        pltpu.VMEM((5, 1, R), jnp.int32),
        pltpu.VMEM((R, R), F32),
        pltpu.VMEM((H, R, SLOTS), BF),
        *[pltpu.VMEM((ng, H, R, HD), F32)] * 4,
        *[pltpu.VMEM((H, R, HD), F32)] * 4,
        *[pltpu.VMEM((HD, SLOTS), F32)] * 2,
        pltpu.VMEM((2, 2, half, width), BF),
        pltpu.VMEM((2, half, width), BF),
        pltpu.VMEM((2, 4, eighth, width), BF),
        pltpu.VMEM((2, 3, eighth, width), BF),
        pltpu.VMEM((2, eighth, width), BF),
        pltpu.VMEM((2, 3, eighth, width), BF),
        pltpu.VMEM((2, 4, eighth, width), BF),
        pltpu.VMEM((2, 2, half, width), BF),
        pltpu.VMEM((3, 8, G), F32),
        pltpu.VMEM((8, G), F32),
        pltpu.VMEM((3, 8, G), F32),
        pltpu.VMEM((3, 8, G), F32),
        pltpu.VMEM((8, R), F32),
        pltpu.VMEM((7, 8, R), F32),
        pltpu.VMEM((5, 2, HD, R), BF),
        pltpu.VMEM((5, 2, HD, R), BF),
        *[pltpu.SemaphoreType.DMA((3, 5))] * 2,
        *[pltpu.SemaphoreType.DMA((2, 11))] * 2,
        *[pltpu.SemaphoreType.DMA((7,))] * 2,
        *[pltpu.SemaphoreType.DMA((7,))] * 2,
        *[pltpu.SemaphoreType.DMA((5,))] * 2,
    ]
    return pl.pallas_call(
        kernel,
        out_shape=(
            jax.ShapeDtypeStruct(queries.shape, BF),
            jax.ShapeDtypeStruct(queries.shape, BF),
            jax.ShapeDtypeStruct(keys.shape, BF),
            jax.ShapeDtypeStruct(values.shape, BF),
        ),
        in_specs=[vmem] * 7,
        out_specs=[vmem] * 4,
        scratch_shapes=scratch,
        compiler_params=pltpu.CompilerParams(
            collective_id=0, has_side_effects=True, vmem_limit_bytes=60 << 20
        ),
        name="butterfly",
    )(
        queries,
        keys,
        values,
        key_keep.reshape(1, R),
        global_positions.reshape(1, G),
        gain.reshape(1, -1),
        cotangent,
    )


def solution(mesh):
    torus = Mesh(mesh.devices.reshape(4, 4, 2, 2, 4), (*SEQ, *HEAD))
    in_specs = (
        P(SEQ, HEAD), P(SEQ, HEAD), P(SEQ, HEAD), P(SEQ), P(), P(HEAD), P(SEQ, HEAD),
    )
    return jax.shard_map(
        per_device,
        mesh=torus,
        in_specs=in_specs,
        out_specs=(P(SEQ, HEAD),) * 4,
        check_vma=False,
    )
```

```python
import functools

import jax
import jax.numpy as jnp
from jax import lax
from jax.experimental import pallas as pl
from jax.experimental.pallas import tpu as pltpu
from jax.sharding import Mesh
from jax.sharding import PartitionSpec as P

HD = 128
FEATURES = 8192
NEG_FILL = -1e30
NORM_EPS = 1e-06
SEQ = ("x", "z", "c")
HEAD = ("zh", "y")
SCALE = HD ** (-0.5)
SCALE2 = SCALE * 1.4426950408889634
F32 = jnp.float32
BF = jnp.bfloat16
H = 8
R = 256
G = 384
SLOTS = 6 * R + G

BLOCKS = [(R * i, R) for i in range(6)] + [(6 * R, G)]
GROUPS = [(0,), (1, 2), (4, 3), (5,), (6,)]


def nt(a, b):
    return lax.dot_general(a, b, (((1,), (1,)), ((), ())), preferred_element_type=F32)


def nn(a, b):
    return jnp.dot(a, b, preferred_element_type=F32)


def tn(a, b):
    return lax.dot_general(a, b, (((0,), (0,)), ((), ())), preferred_element_type=F32)


def wide(x, n):
    return jnp.concatenate([x] * (n // 128), 1)


def head_cols(h):
    return pl.ds(pl.multiple_of(h * HD, HD), HD)


def kernel(
    q_hbm, k_hbm, v_hbm, keep_hbm, gpos_hbm, gain_hbm, ct_hbm,
    normed_ref, dq_ref, dk_ref, dv_ref,
    q_ref, k_ref, v_ref, keep_ref, gpos_ref, gain_ref, ct_ref, in_sems,
    ks, vs, keeps, own_bias, expo, m_s, l_s, o_s, f_s, attn, d_attn, diag, dqs, dks, dvs,
    ga, gc, hb, gx, pb, gz, hfull, full,
    fl, flc, flx, flz,
    gains, squares, crossed, inverse, coef, st, st_in, grad_out, grad_in,
    ring_sem, y_sem, kv_send, kv_recv, g_send, g_recv, f_send, f_recv, st_send, st_recv, gr_send, gr_recv,
):
    x, z, c = lax.axis_index("x"), lax.axis_index("z"), lax.axis_index("c")
    zh, y = lax.axis_index("zh"), lax.axis_index("y")
    x_peers = [lax.rem(x + o, 4) for o in (1, 2, 3)]
    z_peers = [lax.rem(z + o, 4) for o in (1, 2, 3)]
    head_peers = [
        {"zh": lax.rem(zh + dz, 2), "y": lax.rem(y + dy, 4)}
        for dz in range(2)
        for dy in range(4)
        if dz or dy
    ]
    partners = [
        {"c": 1 - c},
        {"z": z + 1 - 2 * lax.rem(z, 2)},
        {"z": lax.rem(z + 2, 4)},
        {"x": x + 1 - 2 * lax.rem(x, 2)},
        {"x": lax.rem(x + 2, 4)},
    ]

    def remote(src, dst, send, recv, device):
        return pltpu.make_async_remote_copy(
            src_ref=src, dst_ref=dst, send_sem=send, recv_sem=recv,
            device_id=device, device_id_type=pl.DeviceIdType.MESH,
        )

    barrier = pltpu.get_barrier_semaphore()
    across = [
        {"zh": lax.div(p, 4), "z": lax.rem(p, 4)}
        for p in (lax.rem(zh * 4 + z + 1, 8), lax.rem(zh * 4 + z + 7, 8))
    ]
    y_peers = [{"y": lax.rem(y + o, 4)} for o in (1, 2, 3)]
    near = [{"c": 1 - c}] + [{"x": p} for p in x_peers] + [{"z": p} for p in z_peers] + y_peers + across

    def signal_all(sem, peers):
        for peer in peers:
            pl.semaphore_signal(sem, inc=1, device_id=peer, device_id_type=pl.DeviceIdType.MESH)

    signal_all(barrier, near)
    inputs = [
        pltpu.make_async_copy(src, dst, in_sems.at[i])
        for i, (src, dst) in enumerate(
            (
                (gpos_hbm, gpos_ref), (k_hbm, k_ref), (v_hbm, v_ref), (keep_hbm, keep_ref),
                (gain_hbm, gain_ref), (q_hbm, q_ref), (ct_hbm, ct_ref),
            )
        )
    ]
    for copy in inputs:
        copy.start()
    for copy in inputs[:4]:
        copy.wait()

    offset = (x * 8 + z * 2 + c) * R
    rows = lax.broadcasted_iota(jnp.int32, (R, G), 0)
    wanted = jnp.concatenate([jnp.broadcast_to(gpos_ref[j : j + 1], (R, HD)) for j in range(G // HD)], 1)
    chosen = (wanted - offset == rows).astype(F32).astype(BF)
    own_kv = jnp.concatenate([k_ref[...], v_ref[...]], 1)
    ga[0] = tn(chosen, own_kv).astype(BF).reshape(2, G // 2, 2 * HD)
    keep_rows = jnp.broadcast_to(keep_ref[...], (8, R)).astype(F32).astype(BF)
    fl[0] = nn(keep_rows, chosen)
    eye = lax.broadcasted_iota(jnp.int32, (R, R), 0) == lax.broadcasted_iota(jnp.int32, (R, R), 1)
    row_bias = jnp.where(jnp.broadcast_to(keep_ref[...], (R, R)) == 1, 0.0, NEG_FILL)
    own_bias[...] = jnp.where(eye, 0.0, row_bias)
    ks[0:R] = k_ref[...]
    vs[0:R] = v_ref[...]

    pl.semaphore_wait(barrier, len(near))
    signal_all(ring_sem, across)

    def kv_copies(b):
        lower = R * (b + 1)
        return [
            remote(k_ref, ks.at[pl.ds(lower, R)], kv_send.at[0, b], kv_recv.at[0, b], partners[b]),
            remote(v_ref, vs.at[pl.ds(lower, R)], kv_send.at[1, b], kv_recv.at[1, b], partners[b]),
            remote(keep_ref, keeps.at[b], kv_send.at[2, b], kv_recv.at[2, b], partners[b]),
        ]

    def started(copies):
        for copy in copies:
            copy.start()
        return copies

    def waited(copies):
        for copy in copies:
            copy.wait()

    def core_stage(t):
        return remote(ga.at[t, 1 - c], gc.at[t], g_send.at[t, 0], g_recv.at[t, 0], {"c": 1 - c})

    def x_stage(t):
        return [
            remote(hb.at[t, p], gx.at[t, i], g_send.at[t, 1 + i], g_recv.at[t, 1 + i], {"x": p})
            for i, p in enumerate(x_peers)
        ]

    def z_stage(t):
        return [
            remote(pb.at[t], gz.at[t, i], g_send.at[t, 4 + i], g_recv.at[t, 4 + i], {"z": p})
            for i, p in enumerate(z_peers)
        ]

    def x_back(t):
        return [
            remote(hfull.at[t, x], hfull.at[t, x], g_send.at[t, 7 + i], g_recv.at[t, 7 + i], {"x": p})
            for i, p in enumerate(x_peers)
        ]

    def core_back(t):
        return remote(full.at[t, c], full.at[t, c], g_send.at[t, 10], g_recv.at[t, 10], {"c": 1 - c})

    def add_core(t):
        total = ga[t, c].astype(F32) + gc[t].astype(F32)
        hb[t] = total.astype(BF).reshape(4, G // 8, 2 * HD)

    def add_x(t):
        total = hb[t, x].astype(F32)
        for i in range(3):
            total = total + gx[t, i].astype(F32)
        pb[t] = total.astype(BF)

    def add_z(t):
        total = pb[t].astype(F32)
        for i in range(3):
            total = total + gz[t, i].astype(F32)
        hfull[t, x] = total.astype(BF)

    def flag_stage(s):
        if s == 0:
            return [remote(fl.at[0], flc, f_send.at[0], f_recv.at[0], {"c": 1 - c})]
        peers = [{"x": p} for p in x_peers] if s == 1 else [{"z": p} for p in z_peers]
        into = flx if s == 1 else flz
        base = 1 if s == 1 else 4
        return [
            remote(fl.at[s], into.at[i], f_send.at[base + i], f_recv.at[base + i], p)
            for i, p in enumerate(peers)
        ]

    def forward_group(g, bias, after=None):
        blocks = [BLOCKS[b] for b in GROUPS[g]]

        def body(h, carry):
            q = q_ref[:, head_cols(h)]
            parts, top = [], None
            for lower, size in blocks:
                s = nt(q, ks[lower : lower + size])
                s = s + (own_bias[...] if lower == 0 else bias[lower])
                parts.append(s)
                for j in range(0, size, 128):
                    piece = s[:, j : j + 128]
                    top = piece if top is None else jnp.maximum(top, piece)
            peak = jnp.broadcast_to(jnp.max(top, 1, keepdims=True), (R, 128)) * SCALE2
            mixed, total = None, None
            for (lower, size), s in zip(blocks, parts):
                e = jnp.exp2(s * SCALE2 - wide(peak, size))
                for j in range(0, size, 128):
                    piece = e[:, j : j + 128]
                    total = piece if total is None else total + piece
                e_bf = e.astype(BF)
                expo[h, :, lower : lower + size] = e_bf
                term = nn(e_bf, vs[lower : lower + size])
                mixed = term if mixed is None else mixed + term
            m_s[g, h] = peak
            l_s[g, h] = jnp.broadcast_to(jnp.sum(total, 1, keepdims=True), (R, 128))
            o_s[g, h] = mixed
            if after is not None:
                after(h)
            return carry

        lax.fori_loop(0, H, body, 0, unroll=2)

    def backward_group(g, before=None):
        blocks = [BLOCKS[b] for b in GROUPS[g]]

        def body(h, carry):
            q = q_ref[:, head_cols(h)]
            if before is not None:
                before(h)
            factor = f_s[g, h]
            grad = (d_attn[h] * factor).astype(BF)
            shift = diag[h] * factor
            q_t, grad_t = q.T, grad.T
            d_query = None
            for lower, size in blocks:
                e = expo[h, :, lower : lower + size]
                d_probs = nt(grad, vs[lower : lower + size])
                d_scores = (e.astype(F32) * (d_probs - wide(shift, size))).astype(BF)
                term = nn(d_scores, ks[lower : lower + size])
                d_query = term if d_query is None else d_query + term
                dks[:, lower : lower + size] += nn(q_t, d_scores)
                dvs[:, lower : lower + size] += nn(grad_t, e)
            if before is not None:
                dqs[h] = d_query
            else:
                dqs[h] += d_query
            return carry

        lax.fori_loop(0, H, body, 0, unroll=2)

    def block_bias(*numbers):
        return {
            BLOCKS[b][0]: jnp.where(keeps[b - 1] == 1, 0.0, NEG_FILL).astype(F32) for b in numbers
        }

    core0 = started([core_stage(0)] + flag_stage(0))
    kv = {b: started(kv_copies(b)) for b in (0, 1)}
    for copy in inputs[4:]:
        copy.wait()
    gains[...] = gain_ref[...].astype(F32)
    waited(core0)
    add_core(0)
    fl[1] = fl[0] + flc[...]
    x0 = started(x_stage(0) + flag_stage(1))
    kv[3] = started(kv_copies(3))
    forward_group(0, {})
    pl.semaphore_wait(ring_sem, 2)
    waited(x0)
    add_x(0)
    fl[2] = fl[1] + flx[0] + flx[1] + flx[2]
    z0 = started(z_stage(0) + flag_stage(2))
    kv[4] = started(kv_copies(4))
    kv[2] = started(kv_copies(2))
    waited(kv[0])
    waited(kv[1])
    forward_group(1, block_bias(1, 2))
    waited(z0)
    signal_all(y_sem, y_peers)
    add_z(0)
    global_keep = fl[2] + flz[0] + flz[1] + flz[2]
    xb0 = started(x_back(0))
    waited(kv[3])
    waited(kv[2])
    forward_group(2, block_bias(4, 3))
    waited(xb0)
    full[0, c] = hfull[0].reshape(G // 2, 2 * HD)
    cb0 = started([core_back(0)])
    waited(kv[4])
    forward_group(3, block_bias(5))
    waited(cb0)
    for half in range(2):
        lower = 6 * R + half * (G // 2)
        ks[lower : lower + G // 2] = full[0, half, :, :HD]
        vs[lower : lower + G // 2] = full[0, half, :, HD:]
    global_bias = jnp.where(global_keep[0:1] > 0.5, 0.0, NEG_FILL)
    pl.semaphore_wait(y_sem, 3)
    squares[...] = jnp.zeros_like(squares)
    crossed[...] = jnp.zeros_like(crossed)

    def merge(h):
        peaks = [m_s[g, h] for g in range(len(GROUPS))]
        peak = functools.reduce(jnp.maximum, peaks)
        weights = [jnp.exp2(p - peak) for p in peaks]
        total = sum(w * l_s[g, h] for g, w in enumerate(weights))
        inv_total = 1.0 / total
        out = None
        for g, w in enumerate(weights):
            factor = w * inv_total
            f_s[g, h] = factor
            term = factor * o_s[g, h]
            out = term if out is None else out + term
        attn[h] = out
        up = ct_ref[:, head_cols(h)].astype(F32) * gains[pl.ds(h, 1)]
        squares[...] += out * out
        crossed[...] += up * out

    forward_group(4, {6 * R: global_bias}, merge)
    rows8 = lax.broadcasted_iota(jnp.int32, (8, R), 0)
    squares_row = jnp.broadcast_to(jnp.sum(squares[...].T, 0, keepdims=True), (8, R))
    crossed_row = jnp.broadcast_to(jnp.sum(crossed[...].T, 0, keepdims=True), (8, R))
    st[...] = jnp.where(rows8 == 0, squares_row, crossed_row)
    stats = started(
        [
            remote(st, st_in.at[i], st_send.at[i], st_recv.at[i], peer)
            for i, peer in enumerate(head_peers)
        ]
    )
    dks[...] = jnp.zeros_like(dks)
    dvs[...] = jnp.zeros_like(dvs)
    waited(stats)
    both = st[...]
    for i in range(7):
        both = both + st_in[i]
    inverse_row = lax.rsqrt(both[0:1] / FEATURES + NORM_EPS)
    coef_row = inverse_row * inverse_row * inverse_row * both[1:2] / FEATURES
    inverse[...] = jnp.broadcast_to(inverse_row, (HD, R)).T
    coef[...] = jnp.broadcast_to(coef_row, (HD, R)).T

    def norm_grad(h):
        out = attn[h]
        up = ct_ref[:, head_cols(h)].astype(F32) * gains[pl.ds(h, 1)]
        grad = inverse[...] * up - out * coef[...]
        d_attn[h] = grad
        diag[h] = jnp.broadcast_to(jnp.sum(grad * out, 1, keepdims=True), (R, HD))

    def send_grads(b):
        lower = R * (b + 1)
        grad_out[b, 0] = (dks[:, lower : lower + R] * SCALE).astype(BF)
        grad_out[b, 1] = dvs[:, lower : lower + R].astype(BF)
        return started(
            [remote(grad_out.at[b], grad_in.at[b], gr_send.at[b], gr_recv.at[b], partners[b])]
        )

    backward_group(4, norm_grad)
    d_global = jnp.concatenate([dks[:, 6 * R :] * SCALE, dvs[:, 6 * R :]], 0).T
    ga[1] = d_global.astype(BF).reshape(2, G // 2, 2 * HD)
    core1 = started([core_stage(1)])
    backward_group(3)
    waited(core1)
    add_core(1)
    x1 = started(x_stage(1))
    sent = send_grads(4)
    backward_group(2)
    waited(x1)
    add_x(1)
    z1 = started(z_stage(1))
    sent += send_grads(2) + send_grads(3)
    backward_group(1)
    waited(z1)
    add_z(1)
    xb1 = started(x_back(1))
    sent += send_grads(1) + send_grads(0)
    backward_group(0)

    def finish(h, carry):
        dq_ref[:, head_cols(h)] = (dqs[h] * SCALE).astype(BF)
        normed_ref[:, head_cols(h)] = (attn[h] * inverse[...] * gains[pl.ds(h, 1)]).astype(BF)
        return carry

    lax.fori_loop(0, H, finish, 0)
    waited(xb1)
    full[1, c] = hfull[1].reshape(G // 2, 2 * HD)
    cb1 = started([core_back(1)])
    waited(sent)
    d_keys = dks[:, 0:R] * SCALE
    d_values = dvs[:, 0:R]
    for b in range(5):
        d_keys = d_keys + grad_in[b, 0].astype(F32)
        d_values = d_values + grad_in[b, 1].astype(F32)
    waited(cb1)
    back = nn(chosen, full[1].reshape(G, 2 * HD))
    dk_ref[...] = (d_keys.T + back[:, :HD]).astype(BF)
    dv_ref[...] = (d_values.T + back[:, HD:]).astype(BF)


def hand_over(*refs):
    sems = refs[8]
    copies = [pltpu.make_async_copy(refs[i], refs[4 + i], sems.at[i]) for i in range(4)]
    for copy in copies:
        copy.start()
    for copy in copies:
        copy.wait()


def per_device(queries, keys, values, key_keep, global_positions, gain, cotangent):
    vmem = pl.BlockSpec(memory_space=pltpu.VMEM)
    ng = len(GROUPS)
    half, eighth, width = G // 2, G // 8, 2 * HD
    scratch = [
        pltpu.VMEM(queries.shape, BF),
        pltpu.VMEM(keys.shape, BF),
        pltpu.VMEM(values.shape, BF),
        pltpu.VMEM((1, R), jnp.int32),
        pltpu.VMEM((G // HD, HD), jnp.int32),
        pltpu.VMEM((H, HD), BF),
        pltpu.VMEM(cotangent.shape, BF),
        pltpu.SemaphoreType.DMA((7,)),
        pltpu.VMEM((SLOTS, HD), BF),
        pltpu.VMEM((SLOTS, HD), BF),
        pltpu.VMEM((5, 1, R), jnp.int32),
        pltpu.VMEM((R, R), F32),
        pltpu.VMEM((H, R, SLOTS), BF),
        *[pltpu.VMEM((ng, H, R, HD), F32)] * 4,
        *[pltpu.VMEM((H, R, HD), F32)] * 4,
        *[pltpu.VMEM((HD, SLOTS), F32)] * 2,
        pltpu.VMEM((2, 2, half, width), BF),
        pltpu.VMEM((2, half, width), BF),
        pltpu.VMEM((2, 4, eighth, width), BF),
        pltpu.VMEM((2, 3, eighth, width), BF),
        pltpu.VMEM((2, eighth, width), BF),
        pltpu.VMEM((2, 3, eighth, width), BF),
        pltpu.VMEM((2, 4, eighth, width), BF),
        pltpu.VMEM((2, 2, half, width), BF),
        pltpu.VMEM((3, 8, G), F32),
        pltpu.VMEM((8, G), F32),
        pltpu.VMEM((3, 8, G), F32),
        pltpu.VMEM((3, 8, G), F32),
        pltpu.VMEM((H, HD), F32),
        *[pltpu.VMEM((R, HD), F32)] * 4,
        pltpu.VMEM((8, R), F32),
        pltpu.VMEM((7, 8, R), F32),
        pltpu.VMEM((5, 2, HD, R), BF),
        pltpu.VMEM((5, 2, HD, R), BF),
        pltpu.SemaphoreType.REGULAR,
        pltpu.SemaphoreType.REGULAR,
        *[pltpu.SemaphoreType.DMA((3, 5))] * 2,
        *[pltpu.SemaphoreType.DMA((2, 11))] * 2,
        *[pltpu.SemaphoreType.DMA((7,))] * 2,
        *[pltpu.SemaphoreType.DMA((7,))] * 2,
        *[pltpu.SemaphoreType.DMA((5,))] * 2,
    ]
    results = pl.pallas_call(
        kernel,
        out_shape=(
            jax.ShapeDtypeStruct(queries.shape, BF),
            jax.ShapeDtypeStruct(queries.shape, BF),
            jax.ShapeDtypeStruct(keys.shape, BF),
            jax.ShapeDtypeStruct(values.shape, BF),
        ),
        in_specs=[pl.BlockSpec(memory_space=pltpu.HBM)] * 7,
        out_specs=[vmem] * 4,
        scratch_shapes=scratch,
        compiler_params=pltpu.CompilerParams(
            collective_id=0, has_side_effects=True, vmem_limit_bytes=42 << 20
        ),
        name="butterfly",
    )(
        *[
            pltpu.with_memory_space_constraint(a, pltpu.HBM)
            for a in (
                queries,
                keys,
                values,
                key_keep.reshape(1, R),
                global_positions.reshape(G // HD, HD),
                gain.reshape(H, HD),
                cotangent,
            )
        ]
    )
    anywhere = pl.BlockSpec(memory_space=pl.ANY)
    return pl.pallas_call(
        hand_over,
        out_shape=tuple(jax.ShapeDtypeStruct(r.shape, r.dtype) for r in results),
        in_specs=[anywhere] * 4,
        out_specs=[anywhere] * 4,
        scratch_shapes=[pltpu.SemaphoreType.DMA((4,))],
        compiler_params=pltpu.CompilerParams(vmem_limit_bytes=1 << 20),
        name="hand_over",
    )(*results)


def solution(mesh):
    torus = Mesh(mesh.devices.reshape(4, 4, 2, 2, 4), (*SEQ, *HEAD))
    in_specs = (
        P(SEQ, HEAD), P(SEQ, HEAD), P(SEQ, HEAD), P(SEQ), P(), P(HEAD), P(SEQ, HEAD),
    )
    return jax.shard_map(
        per_device,
        mesh=torus,
        in_specs=in_specs,
        out_specs=(P(SEQ, HEAD),) * 4,
        check_vma=False,
    )
```

```python
import functools

import jax
import jax.numpy as jnp
from jax import lax
from jax.experimental import pallas as pl
from jax.experimental.pallas import tpu as pltpu
from jax.sharding import Mesh
from jax.sharding import PartitionSpec as P

HD = 128
FEATURES = 8192
NEG_FILL = -1e30
NORM_EPS = 1e-06
SEQ = ("x", "z", "c")
HEAD = ("zh", "y")
SCALE = HD ** (-0.5)
SCALE2 = SCALE * 1.4426950408889634
F32 = jnp.float32
BF = jnp.bfloat16
H = 8
R = 256
G = 384
SLOTS = 6 * R + G

BLOCKS = [(R * i, R) for i in range(6)] + [(6 * R, G)]
GROUPS = [(0, 1), (2, 4), (5, 3), (6,)]


def nt(a, b):
    return lax.dot_general(a, b, (((1,), (1,)), ((), ())), preferred_element_type=F32)


def nn(a, b):
    return jnp.dot(a, b, preferred_element_type=F32)


def tn(a, b):
    return lax.dot_general(a, b, (((0,), (0,)), ((), ())), preferred_element_type=F32)


def wide(x, n):
    return jnp.concatenate([x] * (n // 128), 1)


def head_cols(h):
    return pl.ds(pl.multiple_of(h * HD, HD), HD)


def kernel(
    q_hbm, k_hbm, v_hbm, keep_hbm, gpos_hbm, gain_hbm, ct_hbm,
    normed_ref, dq_ref, dk_ref, dv_ref,
    q_ref, k_ref, v_ref, keep_ref, gpos_ref, gain_ref, ct_ref, in_sems,
    ks, vs, keeps, own_bias, expo, m_s, l_s, o_s, f_s, attn, d_attn, diag, dqs, dks, dvs,
    ga, gx, pb, gz, full, q_t,
    fl, flx, flz,
    gains, squares, crossed, inverse, coef, st, st_in, grad_out, grad_in,
    ring_sem, y_sem, kv_send, kv_recv, g_send, g_recv, f_send, f_recv, st_send, st_recv, gr_send, gr_recv,
):
    x, z, c = lax.axis_index("x"), lax.axis_index("z"), lax.axis_index("c")
    zh, y = lax.axis_index("zh"), lax.axis_index("y")
    plane_peers = [
        {"x": lax.rem(x + dx, 4), "c": c if dc == 0 else 1 - c}
        for dx in (2, 1, 3, 0)
        for dc in range(2)
        if dx or dc
    ]
    me = 2 * x + c
    z_peers = [lax.rem(z + o, 4) for o in (1, 2, 3)]
    head_peers = [
        {"zh": lax.rem(zh + dz, 2), "y": lax.rem(y + dy, 4)}
        for dz in range(2)
        for dy in range(4)
        if dz or dy
    ]
    partners = [
        {"c": 1 - c},
        {"z": z + 1 - 2 * lax.rem(z, 2)},
        {"z": lax.rem(z + 2, 4)},
        {"x": x + 1 - 2 * lax.rem(x, 2)},
        {"x": lax.rem(x + 2, 4)},
    ]

    def remote(src, dst, send, recv, device):
        return pltpu.make_async_remote_copy(
            src_ref=src, dst_ref=dst, send_sem=send, recv_sem=recv,
            device_id=device, device_id_type=pl.DeviceIdType.MESH,
        )

    barrier = pltpu.get_barrier_semaphore()
    across = [
        {"zh": lax.div(p, 4), "z": lax.rem(p, 4)}
        for p in (lax.rem(zh * 4 + z + 1, 8), lax.rem(zh * 4 + z + 7, 8))
    ]
    y_peers = [{"y": lax.rem(y + o, 4)} for o in (1, 2, 3)]
    near = plane_peers + [{"z": p} for p in z_peers] + y_peers + across

    def signal_all(sem, peers):
        for peer in peers:
            pl.semaphore_signal(sem, inc=1, device_id=peer, device_id_type=pl.DeviceIdType.MESH)

    signal_all(barrier, near)
    inputs = [
        pltpu.make_async_copy(src, dst, in_sems.at[i])
        for i, (src, dst) in enumerate(
            (
                (gpos_hbm, gpos_ref), (k_hbm, k_ref), (v_hbm, v_ref), (keep_hbm, keep_ref),
                (gain_hbm, gain_ref), (q_hbm, q_ref), (ct_hbm, ct_ref),
            )
        )
    ]
    for copy in inputs:
        copy.start()
    for copy in inputs[:4]:
        copy.wait()

    offset = (x * 8 + z * 2 + c) * R
    rows = lax.broadcasted_iota(jnp.int32, (R, G), 0)
    wanted = jnp.concatenate([jnp.broadcast_to(gpos_ref[j : j + 1], (R, HD)) for j in range(G // HD)], 1)
    chosen = (wanted - offset == rows).astype(F32).astype(BF)
    own_kv = jnp.concatenate([k_ref[...], v_ref[...]], 1)
    ga[0] = tn(chosen, own_kv).astype(BF).reshape(8, G // 8, 2 * HD)
    keep_rows = jnp.broadcast_to(keep_ref[...], (8, R)).astype(F32).astype(BF)
    fl[0] = nn(keep_rows, chosen)[0:1]
    eye = lax.broadcasted_iota(jnp.int32, (R, R), 0) == lax.broadcasted_iota(jnp.int32, (R, R), 1)
    row_bias = jnp.where(jnp.broadcast_to(keep_ref[...], (R, R)) == 1, 0.0, NEG_FILL)
    own_bias[...] = jnp.where(eye, 0.0, row_bias)
    ks[0:R] = k_ref[...]
    vs[0:R] = v_ref[...]

    pl.semaphore_wait(barrier, len(near))
    signal_all(ring_sem, across)

    def kv_copies(b):
        lower = R * (b + 1)
        return [
            remote(k_ref, ks.at[pl.ds(lower, R)], kv_send.at[0, b], kv_recv.at[0, b], partners[b]),
            remote(v_ref, vs.at[pl.ds(lower, R)], kv_send.at[1, b], kv_recv.at[1, b], partners[b]),
            remote(keep_ref, keeps.at[b], kv_send.at[2, b], kv_recv.at[2, b], partners[b]),
        ]

    def started(copies):
        for copy in copies:
            copy.start()
        return copies

    def waited(copies):
        for copy in copies:
            copy.wait()

    def plane_stage(t):
        return [
            remote(ga.at[t, 2 * p["x"] + p["c"]], gx.at[t, i], g_send.at[t, i], g_recv.at[t, i], p)
            for i, p in enumerate(plane_peers)
        ]

    def z_stage(t):
        return [
            remote(pb.at[t], gz.at[t, i], g_send.at[t, 7 + i], g_recv.at[t, 7 + i], {"z": p})
            for i, p in enumerate(z_peers)
        ]

    def plane_back(t):
        return [
            remote(full.at[t, me], full.at[t, me], g_send.at[t, 10 + i], g_recv.at[t, 10 + i], p)
            for i, p in enumerate(plane_peers)
        ]

    def add_plane(t):
        total = ga[t, me].astype(F32)
        for i in range(7):
            total = total + gx[t, i].astype(F32)
        pb[t] = total.astype(BF)

    def add_z(t):
        total = pb[t].astype(F32)
        for i in range(3):
            total = total + gz[t, i].astype(F32)
        full[t, me] = total.astype(BF)

    def flag_stage(s):
        peers = plane_peers if s == 0 else [{"z": p} for p in z_peers]
        into, base = (flx, 0) if s == 0 else (flz, 7)
        return [
            remote(fl.at[s], into.at[i], f_send.at[base + i], f_recv.at[base + i], p)
            for i, p in enumerate(peers)
        ]

    def forward_group(g, bias, after=None):
        blocks = [BLOCKS[b] for b in GROUPS[g]]

        def body(h, carry):
            q = q_ref[:, head_cols(h)]
            parts, top = [], None
            for lower, size in blocks:
                s = nt(q, ks[lower : lower + size])
                s = s + (own_bias[...] if lower == 0 else bias[lower])
                parts.append(s)
                for j in range(0, size, 128):
                    piece = s[:, j : j + 128]
                    top = piece if top is None else jnp.maximum(top, piece)
            peak = jnp.broadcast_to(jnp.max(top, 1, keepdims=True), (R, 128)) * SCALE2
            mixed, total = None, None
            for (lower, size), s in zip(blocks, parts):
                e = jnp.exp2(s * SCALE2 - wide(peak, size))
                for j in range(0, size, 128):
                    piece = e[:, j : j + 128]
                    total = piece if total is None else total + piece
                e_bf = e.astype(BF)
                expo[h, :, lower : lower + size] = e_bf
                term = nn(e_bf, vs[lower : lower + size])
                mixed = term if mixed is None else mixed + term
            m_s[g, h] = peak
            l_s[g, h] = jnp.broadcast_to(jnp.sum(total, 1, keepdims=True), (R, 128))
            o_s[g, h] = mixed
            if after is not None:
                after(h)
            return carry

        lax.fori_loop(0, H, body, 0, unroll=2)

    def backward_group(g, numbers, before=None):
        blocks = [BLOCKS[b] for b in numbers]

        def body(h, carry):
            if before is not None:
                before(h)
            factor = f_s[g, h]
            grad = (d_attn[h] * factor).astype(BF)
            shift = diag[h] * factor
            grad_t = grad.T
            d_query = None
            for lower, size in blocks:
                e = expo[h, :, lower : lower + size]
                d_probs = nt(grad, vs[lower : lower + size])
                d_scores = (e.astype(F32) * (d_probs - wide(shift, size))).astype(BF)
                term = nn(d_scores, ks[lower : lower + size])
                d_query = term if d_query is None else d_query + term
                dks[:, lower : lower + size] += nn(q_t[h], d_scores)
                dvs[:, lower : lower + size] += nn(grad_t, e)
            if before is not None:
                dqs[h] = d_query
            else:
                dqs[h] += d_query
            return carry

        lax.fori_loop(0, H, body, 0, unroll=2)

    def block_bias(*numbers):
        return {
            BLOCKS[b][0]: jnp.where(keeps[b - 1] == 1, 0.0, NEG_FILL).astype(F32) for b in numbers
        }

    plane0 = started(plane_stage(0) + flag_stage(0))
    kv = {b: started(kv_copies(b)) for b in (0, 1, 3, 4)}
    for copy in inputs[4:]:
        copy.wait()
    gains[...] = gain_ref[...].astype(F32)
    waited(kv[0])
    forward_group(0, block_bias(1))
    pl.semaphore_wait(ring_sem, 2)
    waited(plane0)
    add_plane(0)
    keep_plane = fl[0]
    for i in range(7):
        keep_plane = keep_plane + flx[i]
    fl[1] = keep_plane
    z0 = started(z_stage(0) + flag_stage(1))
    kv[2] = started(kv_copies(2))
    waited(kv[1])
    waited(kv[3])
    forward_group(1, block_bias(2, 4))
    waited(z0)
    signal_all(y_sem, y_peers)
    add_z(0)
    global_keep = fl[1] + flz[0] + flz[1] + flz[2]
    back0 = started(plane_back(0))
    waited(kv[4])
    waited(kv[2])
    forward_group(2, block_bias(5, 3))
    waited(back0)
    lower = 6 * R
    all_kv = full[0].reshape(G, 2 * HD)
    ks[lower : lower + G] = all_kv[:, :HD]
    vs[lower : lower + G] = all_kv[:, HD:]
    global_bias = jnp.where(global_keep[0:1] > 0.5, 0.0, NEG_FILL)
    pl.semaphore_wait(y_sem, 3)
    squares[...] = jnp.zeros_like(squares)
    crossed[...] = jnp.zeros_like(crossed)

    def merge(h):
        peaks = [m_s[g, h] for g in range(len(GROUPS))]
        peak = functools.reduce(jnp.maximum, peaks)
        weights = [jnp.exp2(p - peak) for p in peaks]
        total = sum(w * l_s[g, h] for g, w in enumerate(weights))
        inv_total = 1.0 / total
        out = None
        for g, w in enumerate(weights):
            factor = w * inv_total
            f_s[g, h] = factor
            term = factor * o_s[g, h]
            out = term if out is None else out + term
        attn[h] = out
        up = ct_ref[:, head_cols(h)].astype(F32) * gains[pl.ds(h, 1)]
        squares[...] += out * out
        crossed[...] += up * out

    forward_group(3, {6 * R: global_bias}, merge)
    rows8 = lax.broadcasted_iota(jnp.int32, (8, R), 0)
    squares_row = jnp.broadcast_to(jnp.sum(squares[...].T, 0, keepdims=True), (8, R))
    crossed_row = jnp.broadcast_to(jnp.sum(crossed[...].T, 0, keepdims=True), (8, R))
    st[...] = jnp.where(rows8 == 0, squares_row, crossed_row)
    stats = started(
        [
            remote(st, st_in.at[i], st_send.at[i], st_recv.at[i], peer)
            for i, peer in enumerate(head_peers)
        ]
    )

    def transpose_queries(h, carry):
        q_t[h] = q_ref[:, head_cols(h)].T
        return carry

    lax.fori_loop(0, H, transpose_queries, 0, unroll=2)
    dks[...] = jnp.zeros_like(dks)
    dvs[...] = jnp.zeros_like(dvs)
    waited(stats)
    both = st[...]
    for i in range(7):
        both = both + st_in[i]
    inverse_row = lax.rsqrt(both[0:1] / FEATURES + NORM_EPS)
    coef_row = inverse_row * inverse_row * inverse_row * both[1:2] / FEATURES
    inverse[...] = jnp.broadcast_to(inverse_row, (HD, R)).T
    coef[...] = jnp.broadcast_to(coef_row, (HD, R)).T

    def norm_grad(h):
        out = attn[h]
        up = ct_ref[:, head_cols(h)].astype(F32) * gains[pl.ds(h, 1)]
        grad = inverse[...] * up - out * coef[...]
        d_attn[h] = grad
        diag[h] = jnp.broadcast_to(jnp.sum(grad * out, 1, keepdims=True), (R, HD))

    def send_grads(b):
        lower = R * (b + 1)
        grad_out[b, 0] = (dks[:, lower : lower + R] * SCALE).astype(BF)
        grad_out[b, 1] = dvs[:, lower : lower + R].astype(BF)
        return started(
            [remote(grad_out.at[b], grad_in.at[b], gr_send.at[b], gr_recv.at[b], partners[b])]
        )

    backward_group(3, (6,), norm_grad)
    d_global = jnp.concatenate([dks[:, 6 * R :] * SCALE, dvs[:, 6 * R :]], 0).T
    ga[1] = d_global.astype(BF).reshape(8, G // 8, 2 * HD)
    plane1 = started(plane_stage(1))
    backward_group(2, (5, 3))
    sent = send_grads(4)
    waited(plane1)
    add_plane(1)
    z1 = started(z_stage(1))
    sent += send_grads(2)
    backward_group(1, (4, 2))
    sent += send_grads(3) + send_grads(1)
    waited(z1)
    add_z(1)
    back1 = started(plane_back(1))
    backward_group(0, (1, 0))
    sent += send_grads(0)

    def finish(h, carry):
        dq_ref[:, head_cols(h)] = (dqs[h] * SCALE).astype(BF)
        normed_ref[:, head_cols(h)] = (attn[h] * inverse[...] * gains[pl.ds(h, 1)]).astype(BF)
        return carry

    lax.fori_loop(0, H, finish, 0)
    waited(sent)
    d_keys = dks[:, 0:R] * SCALE
    d_values = dvs[:, 0:R]
    for b in range(5):
        d_keys = d_keys + grad_in[b, 0].astype(F32)
        d_values = d_values + grad_in[b, 1].astype(F32)
    waited(back1)
    back = nn(chosen, full[1].reshape(G, 2 * HD))
    dk_ref[...] = (d_keys.T + back[:, :HD]).astype(BF)
    dv_ref[...] = (d_values.T + back[:, HD:]).astype(BF)


def hand_over(*refs):
    sems = refs[8]
    copies = [pltpu.make_async_copy(refs[i], refs[4 + i], sems.at[i]) for i in range(4)]
    for copy in copies:
        copy.start()
    for copy in copies:
        copy.wait()


def per_device(queries, keys, values, key_keep, global_positions, gain, cotangent):
    vmem = pl.BlockSpec(memory_space=pltpu.VMEM)
    ng = len(GROUPS)
    eighth, width = G // 8, 2 * HD
    scratch = [
        pltpu.VMEM(queries.shape, BF),
        pltpu.VMEM(keys.shape, BF),
        pltpu.VMEM(values.shape, BF),
        pltpu.VMEM((1, R), jnp.int32),
        pltpu.VMEM((G // HD, HD), jnp.int32),
        pltpu.VMEM((H, HD), BF),
        pltpu.VMEM(cotangent.shape, BF),
        pltpu.SemaphoreType.DMA((7,)),
        pltpu.VMEM((SLOTS, HD), BF),
        pltpu.VMEM((SLOTS, HD), BF),
        pltpu.VMEM((5, 1, R), jnp.int32),
        pltpu.VMEM((R, R), F32),
        pltpu.VMEM((H, R, SLOTS), BF),
        *[pltpu.VMEM((ng, H, R, HD), F32)] * 4,
        *[pltpu.VMEM((H, R, HD), F32)] * 4,
        *[pltpu.VMEM((HD, SLOTS), F32)] * 2,
        pltpu.VMEM((2, 8, eighth, width), BF),
        pltpu.VMEM((2, 7, eighth, width), BF),
        pltpu.VMEM((2, eighth, width), BF),
        pltpu.VMEM((2, 3, eighth, width), BF),
        pltpu.VMEM((2, 8, eighth, width), BF),
        pltpu.VMEM((H, HD, R), BF),
        pltpu.VMEM((2, 1, G), F32),
        pltpu.VMEM((7, 1, G), F32),
        pltpu.VMEM((3, 1, G), F32),
        pltpu.VMEM((H, HD), F32),
        *[pltpu.VMEM((R, HD), F32)] * 4,
        pltpu.VMEM((8, R), F32),
        pltpu.VMEM((7, 8, R), F32),
        pltpu.VMEM((5, 2, HD, R), BF),
        pltpu.VMEM((5, 2, HD, R), BF),
        pltpu.SemaphoreType.REGULAR,
        pltpu.SemaphoreType.REGULAR,
        *[pltpu.SemaphoreType.DMA((3, 5))] * 2,
        *[pltpu.SemaphoreType.DMA((2, 17))] * 2,
        *[pltpu.SemaphoreType.DMA((10,))] * 2,
        *[pltpu.SemaphoreType.DMA((7,))] * 2,
        *[pltpu.SemaphoreType.DMA((5,))] * 2,
    ]
    results = pl.pallas_call(
        kernel,
        out_shape=(
            jax.ShapeDtypeStruct(queries.shape, BF),
            jax.ShapeDtypeStruct(queries.shape, BF),
            jax.ShapeDtypeStruct(keys.shape, BF),
            jax.ShapeDtypeStruct(values.shape, BF),
        ),
        in_specs=[pl.BlockSpec(memory_space=pltpu.HBM)] * 7,
        out_specs=[vmem] * 4,
        scratch_shapes=scratch,
        compiler_params=pltpu.CompilerParams(
            collective_id=0, has_side_effects=True, vmem_limit_bytes=42 << 20
        ),
        name="butterfly",
    )(
        *[
            pltpu.with_memory_space_constraint(a, pltpu.HBM)
            for a in (
                queries,
                keys,
                values,
                key_keep.reshape(1, R),
                global_positions.reshape(G // HD, HD),
                gain.reshape(H, HD),
                cotangent,
            )
        ]
    )
    anywhere = pl.BlockSpec(memory_space=pl.ANY)
    return pl.pallas_call(
        hand_over,
        out_shape=tuple(jax.ShapeDtypeStruct(r.shape, r.dtype) for r in results),
        in_specs=[anywhere] * 4,
        out_specs=[anywhere] * 4,
        scratch_shapes=[pltpu.SemaphoreType.DMA((4,))],
        compiler_params=pltpu.CompilerParams(vmem_limit_bytes=1 << 20),
        name="hand_over",
    )(*results)


def solution(mesh):
    torus = Mesh(mesh.devices.reshape(4, 4, 2, 2, 4), (*SEQ, *HEAD))
    in_specs = (
        P(SEQ, HEAD), P(SEQ, HEAD), P(SEQ, HEAD), P(SEQ), P(), P(HEAD), P(SEQ, HEAD),
    )
    return jax.shard_map(
        per_device,
        mesh=torus,
        in_specs=in_specs,
        out_specs=(P(SEQ, HEAD),) * 4,
        check_vma=False,
    )
```

```python
import functools

import jax
import jax.numpy as jnp
from jax import lax
from jax.experimental import pallas as pl
from jax.experimental.pallas import tpu as pltpu
from jax.sharding import Mesh
from jax.sharding import PartitionSpec as P

HD = 128
FEATURES = 8192
NEG_FILL = -1e30
NORM_EPS = 1e-06
SEQ = ("x", "z", "c")
HEAD = ("zh", "y")
SCALE = HD ** (-0.5)
SCALE2 = SCALE * 1.4426950408889634
F32 = jnp.float32
BF = jnp.bfloat16
H = 8
R = 256
G = 384
SLOTS = 6 * R + G

BLOCKS = [(R * i, R) for i in range(6)] + [(6 * R, G)]
GROUPS = [(0, 1), (2, 4), (5, 3), (6,)]


def nt(a, b):
    return lax.dot_general(a, b, (((1,), (1,)), ((), ())), preferred_element_type=F32)


def nn(a, b):
    return jnp.dot(a, b, preferred_element_type=F32)


def tn(a, b):
    return lax.dot_general(a, b, (((0,), (0,)), ((), ())), preferred_element_type=F32)


def wide(x, n):
    return jnp.concatenate([x] * (n // 128), 1)


def head_cols(h):
    return pl.ds(pl.multiple_of(h * HD, HD), HD)


def kernel(
    q_hbm, k_hbm, v_hbm, keep_hbm, gpos_hbm, gain_hbm, ct_hbm,
    normed_ref, dq_ref, dk_ref, dv_ref,
    q_ref, k_ref, v_ref, keep_ref, gpos_ref, gain_ref, ct_ref, in_sems,
    ks, vs, keeps, own_bias, expo, m_s, l_s, o_s, f_s, attn, d_attn, diag, dqs, dks, dvs,
    ga, gx, pb, gz, full, q_t,
    fl, flx, flz,
    up_sums, out_sums, xs, dq2, f_near, gains, squares, crossed, inverse, coef, st, st_in, grad_out, grad_in,
    ring_sem, y_sem, kv_send, kv_recv, g_send, g_recv, f_send, f_recv, st_send, st_recv, gr_send, gr_recv,
):
    x, z, c = lax.axis_index("x"), lax.axis_index("z"), lax.axis_index("c")
    zh, y = lax.axis_index("zh"), lax.axis_index("y")
    plane_peers = [
        {"x": lax.rem(x + dx, 4), "c": c if dc == 0 else 1 - c}
        for dx in (2, 1, 3, 0)
        for dc in range(2)
        if dx or dc
    ]
    me = 2 * x + c
    z_peers = [lax.rem(z + o, 4) for o in (1, 2, 3)]
    head_peers = [
        {"zh": lax.rem(zh + dz, 2), "y": lax.rem(y + dy, 4)}
        for dz in range(2)
        for dy in range(4)
        if dz or dy
    ]
    partners = [
        {"c": 1 - c},
        {"z": z + 1 - 2 * lax.rem(z, 2)},
        {"z": lax.rem(z + 2, 4)},
        {"x": x + 1 - 2 * lax.rem(x, 2)},
        {"x": lax.rem(x + 2, 4)},
    ]

    def remote(src, dst, send, recv, device):
        return pltpu.make_async_remote_copy(
            src_ref=src, dst_ref=dst, send_sem=send, recv_sem=recv,
            device_id=device, device_id_type=pl.DeviceIdType.MESH,
        )

    barrier = pltpu.get_barrier_semaphore()
    across = [
        {"zh": lax.div(p, 4), "z": lax.rem(p, 4)}
        for p in (lax.rem(zh * 4 + z + 1, 8), lax.rem(zh * 4 + z + 7, 8))
    ]
    y_peers = [{"y": lax.rem(y + o, 4)} for o in (1, 2, 3)]
    near = plane_peers + [{"z": p} for p in z_peers] + y_peers + across

    def signal_all(sem, peers):
        for peer in peers:
            pl.semaphore_signal(sem, inc=1, device_id=peer, device_id_type=pl.DeviceIdType.MESH)

    signal_all(barrier, near)
    inputs = [
        pltpu.make_async_copy(src, dst, in_sems.at[i])
        for i, (src, dst) in enumerate(
            (
                (gpos_hbm, gpos_ref), (k_hbm, k_ref), (v_hbm, v_ref), (keep_hbm, keep_ref),
                (gain_hbm, gain_ref), (q_hbm, q_ref), (ct_hbm, ct_ref),
            )
        )
    ]
    for copy in inputs:
        copy.start()
    for copy in inputs[:4]:
        copy.wait()

    offset = (x * 8 + z * 2 + c) * R
    rows = lax.broadcasted_iota(jnp.int32, (R, G), 0)
    wanted = jnp.concatenate([jnp.broadcast_to(gpos_ref[j : j + 1], (R, HD)) for j in range(G // HD)], 1)
    chosen = (wanted - offset == rows).astype(F32).astype(BF)
    own_kv = jnp.concatenate([k_ref[...], v_ref[...]], 1)
    ga[0] = tn(chosen, own_kv).astype(BF).reshape(8, G // 8, 2 * HD)
    keep_rows = jnp.broadcast_to(keep_ref[...], (8, R)).astype(F32).astype(BF)
    fl[0] = nn(keep_rows, chosen)[0:1]
    eye = lax.broadcasted_iota(jnp.int32, (R, R), 0) == lax.broadcasted_iota(jnp.int32, (R, R), 1)
    row_bias = jnp.where(jnp.broadcast_to(keep_ref[...], (R, R)) == 1, 0.0, NEG_FILL)
    own_bias[...] = jnp.where(eye, 0.0, row_bias)
    ks[0:R] = k_ref[...]
    vs[0:R] = v_ref[...]

    pl.semaphore_wait(barrier, len(near))
    signal_all(ring_sem, across)

    def kv_copies(b):
        lower = R * (b + 1)
        return [
            remote(k_ref, ks.at[pl.ds(lower, R)], kv_send.at[0, b], kv_recv.at[0, b], partners[b]),
            remote(v_ref, vs.at[pl.ds(lower, R)], kv_send.at[1, b], kv_recv.at[1, b], partners[b]),
            remote(keep_ref, keeps.at[b], kv_send.at[2, b], kv_recv.at[2, b], partners[b]),
        ]

    def started(copies):
        for copy in copies:
            copy.start()
        return copies

    def waited(copies):
        for copy in copies:
            copy.wait()

    def plane_stage(t):
        return [
            remote(ga.at[t, 2 * p["x"] + p["c"]], gx.at[t, i], g_send.at[t, i], g_recv.at[t, i], p)
            for i, p in enumerate(plane_peers)
        ]

    def z_stage(t):
        return [
            remote(pb.at[t], gz.at[t, i], g_send.at[t, 7 + i], g_recv.at[t, 7 + i], {"z": p})
            for i, p in enumerate(z_peers)
        ]

    def plane_back(t):
        return [
            remote(full.at[t, me], full.at[t, me], g_send.at[t, 10 + i], g_recv.at[t, 10 + i], p)
            for i, p in enumerate(plane_peers)
        ]

    def add_plane(t):
        total = ga[t, me].astype(F32)
        for i in range(7):
            total = total + gx[t, i].astype(F32)
        pb[t] = total.astype(BF)

    def add_z(t):
        total = pb[t].astype(F32)
        for i in range(3):
            total = total + gz[t, i].astype(F32)
        full[t, me] = total.astype(BF)

    def flag_stage(s):
        peers = plane_peers if s == 0 else [{"z": p} for p in z_peers]
        into, base = (flx, 0) if s == 0 else (flz, 7)
        return [
            remote(fl.at[s], into.at[i], f_send.at[base + i], f_recv.at[base + i], p)
            for i, p in enumerate(peers)
        ]

    def forward_group(g, bias, after=None):
        blocks = [BLOCKS[b] for b in GROUPS[g]]

        def body(h, carry):
            q = q_ref[:, head_cols(h)]
            parts, top = [], None
            for lower, size in blocks:
                s = nt(q, ks[lower : lower + size])
                s = s + (own_bias[...] if lower == 0 else bias[lower])
                parts.append(s)
                for j in range(0, size, 128):
                    piece = s[:, j : j + 128]
                    top = piece if top is None else jnp.maximum(top, piece)
            peak = jnp.broadcast_to(jnp.max(top, 1, keepdims=True), (R, 128)) * SCALE2
            mixed, total = None, None
            for (lower, size), s in zip(blocks, parts):
                e = jnp.exp2(s * SCALE2 - wide(peak, size))
                for j in range(0, size, 128):
                    piece = e[:, j : j + 128]
                    total = piece if total is None else total + piece
                e_bf = e.astype(BF)
                expo[h, :, lower : lower + size] = e_bf
                term = nn(e_bf, vs[lower : lower + size])
                mixed = term if mixed is None else mixed + term
            m_s[g, h] = peak
            l_s[g, h] = jnp.broadcast_to(jnp.sum(total, 1, keepdims=True), (R, 128))
            o_s[g, h] = mixed
            if after is not None:
                after(h)
            return carry

        lax.fori_loop(0, H, body, 0, unroll=2)

    def backward_group(g, numbers, first=False):
        blocks = [BLOCKS[b] for b in numbers]

        def body(h, carry):
            factor = f_s[g, h]
            grad = (d_attn[h] * factor).astype(BF)
            shift = diag[h] * factor
            grad_t = grad.T
            d_query = None
            for lower, size in blocks:
                e = expo[h, :, lower : lower + size]
                d_probs = nt(grad, vs[lower : lower + size])
                d_scores = (e.astype(F32) * (d_probs - wide(shift, size))).astype(BF)
                term = nn(d_scores, ks[lower : lower + size])
                d_query = term if d_query is None else d_query + term
                dks[:, lower : lower + size] += nn(q_t[h], d_scores)
                dvs[:, lower : lower + size] += nn(grad_t, e)
            if first:
                dqs[h] = inverse[...] * dqs[h] - coef[...] * dq2[h] + d_query
            else:
                dqs[h] += d_query
            return carry

        lax.fori_loop(0, H, body, 0, unroll=2)

    def block_bias(*numbers):
        return {
            BLOCKS[b][0]: jnp.where(keeps[b - 1] == 1, 0.0, NEG_FILL).astype(F32) for b in numbers
        }

    plane0 = started(plane_stage(0) + flag_stage(0))
    kv = {b: started(kv_copies(b)) for b in (0, 2, 3, 1, 4)}
    for copy in inputs[4:]:
        copy.wait()
    gains[...] = gain_ref[...].astype(F32)
    waited(kv[0])
    forward_group(0, block_bias(1))
    pl.semaphore_wait(ring_sem, 2)
    waited(plane0)
    add_plane(0)
    keep_plane = fl[0]
    for i in range(7):
        keep_plane = keep_plane + flx[i]
    fl[1] = keep_plane
    z0 = started(z_stage(0) + flag_stage(1))
    waited(kv[1])
    waited(kv[3])
    forward_group(1, block_bias(2, 4))
    waited(z0)
    signal_all(y_sem, y_peers)
    add_z(0)
    global_keep = fl[1] + flz[0] + flz[1] + flz[2]
    back0 = started(plane_back(0))
    waited(kv[4])
    waited(kv[2])
    forward_group(2, block_bias(5, 3))

    def merge_near(h, carry):
        peaks = [m_s[g, h] for g in range(3)]
        peak = functools.reduce(jnp.maximum, peaks)
        total, out = None, None
        for g, p in enumerate(peaks):
            weight = jnp.exp2(p - peak)
            f_s[g, h] = weight
            total = weight * l_s[g, h] if g == 0 else total + weight * l_s[g, h]
            out = weight * o_s[g, h] if g == 0 else out + weight * o_s[g, h]
        m_s[0, h], l_s[0, h], o_s[0, h] = peak, total, out
        return carry

    lax.fori_loop(0, H, merge_near, 0)
    waited(back0)
    lower = 6 * R
    all_kv = full[0].reshape(G, 2 * HD)
    ks[lower : lower + G] = all_kv[:, :HD]
    vs[lower : lower + G] = all_kv[:, HD:]
    global_bias = jnp.where(global_keep[0:1] > 0.5, 0.0, NEG_FILL)
    pl.semaphore_wait(y_sem, 3)
    squares[...] = jnp.zeros_like(squares)
    crossed[...] = jnp.zeros_like(crossed)

    def merge(h):
        peak = jnp.maximum(m_s[0, h], m_s[3, h])
        near_weight, far_weight = jnp.exp2(m_s[0, h] - peak), jnp.exp2(m_s[3, h] - peak)
        inv_total = 1.0 / (near_weight * l_s[0, h] + far_weight * l_s[3, h])
        near_weight, far_weight = near_weight * inv_total, far_weight * inv_total
        f_near[h] = near_weight
        f_s[3, h] = far_weight
        out = near_weight * o_s[0, h] + far_weight * o_s[3, h]
        attn[h] = out
        up = ct_ref[:, head_cols(h)].astype(F32) * gains[pl.ds(h, 1)]
        squares[...] += out * out
        crossed[...] += up * out

    forward_group(3, {6 * R: global_bias}, merge)
    rows8 = lax.broadcasted_iota(jnp.int32, (8, R), 0)
    squares_row = jnp.broadcast_to(jnp.sum(squares[...].T, 0, keepdims=True), (8, R))
    crossed_row = jnp.broadcast_to(jnp.sum(crossed[...].T, 0, keepdims=True), (8, R))
    st[...] = jnp.where(rows8 == 0, squares_row, crossed_row)
    stats = started(
        [
            remote(st, st_in.at[i], st_send.at[i], st_recv.at[i], peer)
            for i, peer in enumerate(head_peers)
        ]
    )

    def prepare(h, carry):
        q_t[h] = q_ref[:, head_cols(h)].T
        for g in range(3):
            f_s[g, h] = f_s[g, h] * f_near[h]
        factor, out = f_s[3, h], attn[h]
        up = ct_ref[:, head_cols(h)].astype(F32) * gains[pl.ds(h, 1)]
        up_sum = jnp.broadcast_to(jnp.sum(up * out, 1, keepdims=True), (R, HD))
        out_sum = jnp.broadcast_to(jnp.sum(out * out, 1, keepdims=True), (R, HD))
        up_sums[h], out_sums[h] = up_sum, out_sum
        e = expo[h, :, 6 * R :].astype(F32)
        x1 = (e * (nt((up * factor).astype(BF), vs[6 * R :]) - wide(up_sum * factor, G))).astype(BF)
        x2 = (e * (nt((out * factor).astype(BF), vs[6 * R :]) - wide(out_sum * factor, G))).astype(BF)
        xs[h, 0:R], xs[h, R : 2 * R] = x1, x2
        dqs[h] = nn(x1, ks[6 * R :])
        dq2[h] = nn(x2, ks[6 * R :])
        return carry

    lax.fori_loop(0, H, prepare, 0, unroll=2)
    dks[...] = jnp.zeros_like(dks)
    dvs[...] = jnp.zeros_like(dvs)
    waited(stats)
    both = st[...]
    for i in range(7):
        both = both + st_in[i]
    inverse_row = lax.rsqrt(both[0:1] / FEATURES + NORM_EPS)
    coef_row = inverse_row * inverse_row * inverse_row * both[1:2] / FEATURES
    inverse[...] = jnp.broadcast_to(inverse_row, (HD, R)).T
    coef[...] = jnp.broadcast_to(coef_row, (HD, R)).T

    inverse_t = jnp.broadcast_to(inverse_row, (HD, R))
    coef_t = jnp.broadcast_to(-coef_row, (HD, R))

    def global_grads(h, carry):
        out = attn[h]
        up = ct_ref[:, head_cols(h)].astype(F32) * gains[pl.ds(h, 1)]
        grad = inverse[...] * up - out * coef[...]
        d_attn[h] = grad
        diag[h] = inverse[...] * up_sums[h] - coef[...] * out_sums[h]
        queries = q_t[h].astype(F32)
        both_t = jnp.concatenate([queries * inverse_t, queries * coef_t], 1).astype(BF)
        dks[:, 6 * R :] += nn(both_t, xs[h])
        grad_t = (grad * f_s[3, h]).astype(BF).T
        dvs[:, 6 * R :] += nn(grad_t, expo[h, :, 6 * R :])
        return carry

    def send_grads(b):
        lower = R * (b + 1)
        grad_out[b, 0] = (dks[:, lower : lower + R] * SCALE).astype(BF)
        grad_out[b, 1] = dvs[:, lower : lower + R].astype(BF)
        return started(
            [remote(grad_out.at[b], grad_in.at[b], gr_send.at[b], gr_recv.at[b], partners[b])]
        )

    lax.fori_loop(0, H, global_grads, 0, unroll=2)
    d_global = jnp.concatenate([dks[:, 6 * R :] * SCALE, dvs[:, 6 * R :]], 0).astype(BF).T
    ga[1] = d_global.reshape(8, G // 8, 2 * HD)
    plane1 = started(plane_stage(1))
    backward_group(2, (5, 3), True)
    sent = send_grads(4)
    waited(plane1)
    add_plane(1)
    z1 = started(z_stage(1))
    sent += send_grads(2)
    backward_group(1, (4, 2))
    sent += send_grads(3) + send_grads(1)
    waited(z1)
    add_z(1)
    back1 = started(plane_back(1))
    backward_group(0, (1, 0))
    sent += send_grads(0)

    def finish(h, carry):
        dq_ref[:, head_cols(h)] = (dqs[h] * SCALE).astype(BF)
        normed_ref[:, head_cols(h)] = (attn[h] * inverse[...] * gains[pl.ds(h, 1)]).astype(BF)
        return carry

    lax.fori_loop(0, H, finish, 0)
    waited(sent)
    d_keys = dks[:, 0:R] * SCALE
    d_values = dvs[:, 0:R]
    for b in range(5):
        d_keys = d_keys + grad_in[b, 0].astype(F32)
        d_values = d_values + grad_in[b, 1].astype(F32)
    waited(back1)
    back = nn(chosen, full[1].reshape(G, 2 * HD))
    dk_ref[...] = (d_keys.T + back[:, :HD]).astype(BF)
    dv_ref[...] = (d_values.T + back[:, HD:]).astype(BF)


def hand_over(*refs):
    sems = refs[8]
    copies = [pltpu.make_async_copy(refs[i], refs[4 + i], sems.at[i]) for i in range(4)]
    for copy in copies:
        copy.start()
    for copy in copies:
        copy.wait()


def per_device(queries, keys, values, key_keep, global_positions, gain, cotangent):
    vmem = pl.BlockSpec(memory_space=pltpu.VMEM)
    ng = len(GROUPS)
    eighth, width = G // 8, 2 * HD
    scratch = [
        pltpu.VMEM(queries.shape, BF),
        pltpu.VMEM(keys.shape, BF),
        pltpu.VMEM(values.shape, BF),
        pltpu.VMEM((1, R), jnp.int32),
        pltpu.VMEM((G // HD, HD), jnp.int32),
        pltpu.VMEM((H, HD), BF),
        pltpu.VMEM(cotangent.shape, BF),
        pltpu.SemaphoreType.DMA((7,)),
        pltpu.VMEM((SLOTS, HD), BF),
        pltpu.VMEM((SLOTS, HD), BF),
        pltpu.VMEM((5, 1, R), jnp.int32),
        pltpu.VMEM((R, R), F32),
        pltpu.VMEM((H, R, SLOTS), BF),
        *[pltpu.VMEM((ng, H, R, HD), F32)] * 4,
        *[pltpu.VMEM((H, R, HD), F32)] * 4,
        *[pltpu.VMEM((HD, SLOTS), F32)] * 2,
        pltpu.VMEM((2, 8, eighth, width), BF),
        pltpu.VMEM((2, 7, eighth, width), BF),
        pltpu.VMEM((2, eighth, width), BF),
        pltpu.VMEM((2, 3, eighth, width), BF),
        pltpu.VMEM((2, 8, eighth, width), BF),
        pltpu.VMEM((H, HD, R), BF),
        pltpu.VMEM((2, 1, G), F32),
        pltpu.VMEM((7, 1, G), F32),
        pltpu.VMEM((3, 1, G), F32),
        *[pltpu.VMEM((H, R, HD), F32)] * 2,
        pltpu.VMEM((H, 2 * R, G), BF),
        *[pltpu.VMEM((H, R, HD), F32)] * 2,
        pltpu.VMEM((H, HD), F32),
        *[pltpu.VMEM((R, HD), F32)] * 4,
        pltpu.VMEM((8, R), F32),
        pltpu.VMEM((7, 8, R), F32),
        pltpu.VMEM((5, 2, HD, R), BF),
        pltpu.VMEM((5, 2, HD, R), BF),
        pltpu.SemaphoreType.REGULAR,
        pltpu.SemaphoreType.REGULAR,
        *[pltpu.SemaphoreType.DMA((3, 5))] * 2,
        *[pltpu.SemaphoreType.DMA((2, 17))] * 2,
        *[pltpu.SemaphoreType.DMA((10,))] * 2,
        *[pltpu.SemaphoreType.DMA((7,))] * 2,
        *[pltpu.SemaphoreType.DMA((5,))] * 2,
    ]
    results = pl.pallas_call(
        kernel,
        out_shape=(
            jax.ShapeDtypeStruct(queries.shape, BF),
            jax.ShapeDtypeStruct(queries.shape, BF),
            jax.ShapeDtypeStruct(keys.shape, BF),
            jax.ShapeDtypeStruct(values.shape, BF),
        ),
        in_specs=[pl.BlockSpec(memory_space=pltpu.HBM)] * 7,
        out_specs=[vmem] * 4,
        scratch_shapes=scratch,
        compiler_params=pltpu.CompilerParams(
            collective_id=0, has_side_effects=True, vmem_limit_bytes=46 << 20
        ),
        name="butterfly",
    )(
        *[
            pltpu.with_memory_space_constraint(a, pltpu.HBM)
            for a in (
                queries,
                keys,
                values,
                key_keep.reshape(1, R),
                global_positions.reshape(G // HD, HD),
                gain.reshape(H, HD),
                cotangent,
            )
        ]
    )
    anywhere = pl.BlockSpec(memory_space=pl.ANY)
    return pl.pallas_call(
        hand_over,
        out_shape=tuple(jax.ShapeDtypeStruct(r.shape, r.dtype) for r in results),
        in_specs=[anywhere] * 4,
        out_specs=[anywhere] * 4,
        scratch_shapes=[pltpu.SemaphoreType.DMA((4,))],
        compiler_params=pltpu.CompilerParams(vmem_limit_bytes=1 << 20),
        name="hand_over",
    )(*results)


def solution(mesh):
    torus = Mesh(mesh.devices.reshape(4, 4, 2, 2, 4), (*SEQ, *HEAD))
    in_specs = (
        P(SEQ, HEAD), P(SEQ, HEAD), P(SEQ, HEAD), P(SEQ), P(), P(HEAD), P(SEQ, HEAD),
    )
    return jax.shard_map(
        per_device,
        mesh=torus,
        in_specs=in_specs,
        out_specs=(P(SEQ, HEAD),) * 4,
        check_vma=False,
    )
```

```python
import functools

import jax
import jax.numpy as jnp
from jax import lax
from jax.experimental import pallas as pl
from jax.experimental.pallas import tpu as pltpu
from jax.sharding import Mesh
from jax.sharding import PartitionSpec as P

HD = 128
FEATURES = 8192
NEG_FILL = -1e30
NORM_EPS = 1e-06
SEQ = ("x", "z", "c")
HEAD = ("zh", "y")
SCALE = HD ** (-0.5)
SCALE2 = SCALE * 1.4426950408889634
F32 = jnp.float32
BF = jnp.bfloat16
H = 8
R = 256
G = 384
SLOTS = 6 * R + G

BLOCKS = [(R * i, R) for i in range(6)] + [(6 * R, G)]
GROUPS = [(0, 1), (3, 2), (5, 4), (6,)]


def nt(a, b):
    return lax.dot_general(a, b, (((1,), (1,)), ((), ())), preferred_element_type=F32)


def nn(a, b):
    return jnp.dot(a, b, preferred_element_type=F32)


def tn(a, b):
    return lax.dot_general(a, b, (((0,), (0,)), ((), ())), preferred_element_type=F32)


def wide(x, n):
    return jnp.concatenate([x] * (n // 128), 1)


def head_cols(h):
    return pl.ds(pl.multiple_of(h * HD, HD), HD)


def kernel(
    q_hbm, k_hbm, v_hbm, keep_hbm, gpos_hbm, gain_hbm, ct_hbm,
    normed_ref, dq_ref, dk_ref, dv_ref,
    q_ref, k_ref, v_ref, keep_ref, gpos_ref, gain_ref, ct_ref, in_sems,
    ks, vs, keeps, own_bias, expo, m_s, l_s, o_s, f_s, attn, d_attn, diag, dqs, dks, dvs,
    ga, gx, pb, gz, full, q_t,
    fl, flx, flz,
    up_sums, out_sums, xs, dq2, f_near, gains, squares, crossed, inverse, coef, st, st_in, grad_out, grad_in,
    ring_sem, y_sem, kv_send, kv_recv, g_send, g_recv, f_send, f_recv, st_send, st_recv, gr_send, gr_recv,
):
    x, z, c = lax.axis_index("x"), lax.axis_index("z"), lax.axis_index("c")
    zh, y = lax.axis_index("zh"), lax.axis_index("y")
    plane_peers = [
        {"x": lax.rem(x + dx, 4), "c": c if dc == 0 else 1 - c}
        for dx in (2, 1, 3, 0)
        for dc in range(2)
        if dx or dc
    ]
    me = 2 * x + c
    z_peers = [lax.rem(z + o, 4) for o in (1, 2, 3)]
    head_peers = [
        {"zh": lax.rem(zh + dz, 2), "y": lax.rem(y + dy, 4)}
        for dz in range(2)
        for dy in range(4)
        if dz or dy
    ]
    partners = [
        {"c": 1 - c},
        {"z": z + 1 - 2 * lax.rem(z, 2)},
        {"z": lax.rem(z + 2, 4)},
        {"x": x + 1 - 2 * lax.rem(x, 2)},
        {"x": lax.rem(x + 2, 4)},
    ]

    def remote(src, dst, send, recv, device):
        return pltpu.make_async_remote_copy(
            src_ref=src, dst_ref=dst, send_sem=send, recv_sem=recv,
            device_id=device, device_id_type=pl.DeviceIdType.MESH,
        )

    barrier = pltpu.get_barrier_semaphore()
    across = [
        {"zh": lax.div(p, 4), "z": lax.rem(p, 4)}
        for p in (lax.rem(zh * 4 + z + 1, 8), lax.rem(zh * 4 + z + 7, 8))
    ]
    y_peers = [{"y": lax.rem(y + o, 4)} for o in (1, 2, 3)]
    near = plane_peers + [{"z": p} for p in z_peers] + y_peers + across

    def signal_all(sem, peers):
        for peer in peers:
            pl.semaphore_signal(sem, inc=1, device_id=peer, device_id_type=pl.DeviceIdType.MESH)

    signal_all(barrier, near)
    inputs = [
        pltpu.make_async_copy(src, dst, in_sems.at[i])
        for i, (src, dst) in enumerate(
            (
                (gpos_hbm, gpos_ref), (k_hbm, k_ref), (v_hbm, v_ref), (keep_hbm, keep_ref),
                (gain_hbm, gain_ref), (q_hbm, q_ref), (ct_hbm, ct_ref),
            )
        )
    ]
    for copy in inputs:
        copy.start()
    for copy in inputs[:4]:
        copy.wait()

    offset = (x * 8 + z * 2 + c) * R
    rows = lax.broadcasted_iota(jnp.int32, (R, G), 0)
    wanted = jnp.concatenate([jnp.broadcast_to(gpos_ref[j : j + 1], (R, HD)) for j in range(G // HD)], 1)
    chosen = (wanted - offset == rows).astype(F32).astype(BF)
    own_kv = jnp.concatenate([k_ref[...], v_ref[...]], 1)
    ga[0] = tn(chosen, own_kv).astype(BF).reshape(8, G // 8, 2 * HD)
    keep_rows = jnp.broadcast_to(keep_ref[...], (8, R)).astype(F32).astype(BF)
    fl[0] = nn(keep_rows, chosen)[0:1]
    eye = lax.broadcasted_iota(jnp.int32, (R, R), 0) == lax.broadcasted_iota(jnp.int32, (R, R), 1)
    row_bias = jnp.where(jnp.broadcast_to(keep_ref[...], (R, R)) == 1, 0.0, NEG_FILL)
    own_bias[...] = jnp.where(eye, 0.0, row_bias)
    ks[0:R] = k_ref[...]
    vs[0:R] = v_ref[...]

    pl.semaphore_wait(barrier, len(near))
    signal_all(ring_sem, across)

    def kv_copies(b):
        lower = R * (b + 1)
        return [
            remote(k_ref, ks.at[pl.ds(lower, R)], kv_send.at[0, b], kv_recv.at[0, b], partners[b]),
            remote(v_ref, vs.at[pl.ds(lower, R)], kv_send.at[1, b], kv_recv.at[1, b], partners[b]),
            remote(keep_ref, keeps.at[b], kv_send.at[2, b], kv_recv.at[2, b], partners[b]),
        ]

    def started(copies):
        for copy in copies:
            copy.start()
        return copies

    def waited(copies):
        for copy in copies:
            copy.wait()

    def plane_stage(t):
        return [
            remote(ga.at[t, 2 * p["x"] + p["c"]], gx.at[t, i], g_send.at[t, i], g_recv.at[t, i], p)
            for i, p in enumerate(plane_peers)
        ]

    def z_stage(t):
        return [
            remote(pb.at[t], gz.at[t, i], g_send.at[t, 7 + i], g_recv.at[t, 7 + i], {"z": p})
            for i, p in enumerate(z_peers)
        ]

    def plane_back(t):
        return [
            remote(full.at[t, me], full.at[t, me], g_send.at[t, 10 + i], g_recv.at[t, 10 + i], p)
            for i, p in enumerate(plane_peers)
        ]

    def add_plane(t):
        total = ga[t, me].astype(F32)
        for i in range(7):
            total = total + gx[t, i].astype(F32)
        pb[t] = total.astype(BF)

    def add_z(t):
        total = pb[t].astype(F32)
        for i in range(3):
            total = total + gz[t, i].astype(F32)
        full[t, me] = total.astype(BF)

    def flag_stage(s):
        peers = plane_peers if s == 0 else [{"z": p} for p in z_peers]
        into, base = (flx, 0) if s == 0 else (flz, 7)
        return [
            remote(fl.at[s], into.at[i], f_send.at[base + i], f_recv.at[base + i], p)
            for i, p in enumerate(peers)
        ]

    def forward_group(g, bias, after=None, heads=2):
        blocks = [BLOCKS[b] for b in GROUPS[g]]

        def body(i, carry):
            hs = [heads * i + j for j in range(heads)]
            queries = [q_ref[:, head_cols(h)] for h in hs]
            given = [after[0](h) for h in hs] if after is not None else None
            scores = []
            for q in queries:
                parts = []
                for lower, size in blocks:
                    s = nt(q, ks[lower : lower + size])
                    parts.append(s + (own_bias[...] if lower == 0 else bias[lower]))
                scores.append(parts)
            results = []
            for parts in scores:
                top = None
                for s in parts:
                    for j in range(0, s.shape[1], 128):
                        piece = s[:, j : j + 128]
                        top = piece if top is None else jnp.maximum(top, piece)
                peak = jnp.broadcast_to(jnp.max(top, 1, keepdims=True), (R, 128)) * SCALE2
                mixed, total, expos = None, None, []
                for (lower, size), s in zip(blocks, parts):
                    e = jnp.exp2(s * SCALE2 - wide(peak, size))
                    for j in range(0, size, 128):
                        piece = e[:, j : j + 128]
                        total = piece if total is None else total + piece
                    e_bf = e.astype(BF)
                    expos.append(e_bf)
                    term = nn(e_bf, vs[lower : lower + size])
                    mixed = term if mixed is None else mixed + term
                total = jnp.broadcast_to(jnp.sum(total, 1, keepdims=True), (R, 128))
                results.append((peak, total, mixed, expos))
            for h, (peak, total, mixed, expos) in zip(hs, results):
                for (lower, size), e_bf in zip(blocks, expos):
                    expo[h, :, lower : lower + size] = e_bf
                if after is None:
                    m_s[g, h], l_s[g, h], o_s[g, h] = peak, total, mixed
            if after is not None:
                after[1](hs, given, results)
            return carry

        lax.fori_loop(0, H // heads, body, 0)

    def backward_group(g, numbers, first=False):
        blocks = [BLOCKS[b] for b in numbers]

        def body(h, carry):
            factor = f_s[g, h]
            grad = (d_attn[h] * factor).astype(BF)
            shift = diag[h] * factor
            grad_t = grad.T
            d_query = None
            for lower, size in blocks:
                e = expo[h, :, lower : lower + size]
                d_probs = nt(grad, vs[lower : lower + size])
                d_scores = (e.astype(F32) * (d_probs - wide(shift, size))).astype(BF)
                term = nn(d_scores, ks[lower : lower + size])
                d_query = term if d_query is None else d_query + term
                dks[:, lower : lower + size] += nn(q_t[h], d_scores)
                dvs[:, lower : lower + size] += nn(grad_t, e)
            if first:
                dqs[h] = inverse[...] * dqs[h] - coef[...] * dq2[h] + d_query
            else:
                dqs[h] += d_query
            return carry

        lax.fori_loop(0, H, body, 0, unroll=2)

    def block_bias(*numbers):
        return {
            BLOCKS[b][0]: jnp.where(keeps[b - 1] == 1, 0.0, NEG_FILL).astype(F32) for b in numbers
        }

    plane0 = started(plane_stage(0) + flag_stage(0))
    kv = {b: started(kv_copies(b)) for b in (0, 2, 3, 1, 4)}
    for copy in inputs[4:]:
        copy.wait()
    gains[...] = gain_ref[...].astype(F32)
    waited(kv[0])
    forward_group(0, block_bias(1))
    pl.semaphore_wait(ring_sem, 2)
    waited(plane0)
    add_plane(0)
    keep_plane = fl[0]
    for i in range(7):
        keep_plane = keep_plane + flx[i]
    fl[1] = keep_plane
    z0 = started(z_stage(0) + flag_stage(1))
    waited(kv[2])
    waited(kv[1])
    forward_group(1, block_bias(3, 2))
    waited(z0)
    signal_all(y_sem, y_peers)
    add_z(0)
    global_keep = fl[1] + flz[0] + flz[1] + flz[2]
    back0 = started(plane_back(0))
    waited(kv[3])
    waited(kv[4])
    forward_group(2, block_bias(5, 4))

    def merge_near(h, carry):
        peaks = [m_s[g, h] for g in range(3)]
        peak = functools.reduce(jnp.maximum, peaks)
        total, out = None, None
        for g, p in enumerate(peaks):
            weight = jnp.exp2(p - peak)
            f_s[g, h] = weight
            total = weight * l_s[g, h] if g == 0 else total + weight * l_s[g, h]
            out = weight * o_s[g, h] if g == 0 else out + weight * o_s[g, h]
        m_s[0, h], l_s[0, h], o_s[0, h] = peak, total, out
        return carry

    lax.fori_loop(0, H, merge_near, 0)
    waited(back0)
    lower = 6 * R
    all_kv = full[0].reshape(G, 2 * HD)
    ks[lower : lower + G] = all_kv[:, :HD]
    vs[lower : lower + G] = all_kv[:, HD:]
    global_bias = jnp.where(global_keep[0:1] > 0.5, 0.0, NEG_FILL)
    pl.semaphore_wait(y_sem, 3)
    squares[...] = jnp.zeros_like(squares)
    crossed[...] = jnp.zeros_like(crossed)

    def merge_load(h):
        up = ct_ref[:, head_cols(h)].astype(F32) * gains[pl.ds(h, 1)]
        return m_s[0, h], l_s[0, h], o_s[0, h], up

    def merge(hs, given, results):
        square, cross, kept = None, None, []
        for (m0, l0, o0, up), (m3, l3, o3, _) in zip(given, results):
            peak = jnp.maximum(m0, m3)
            near_weight, far_weight = jnp.exp2(m0 - peak), jnp.exp2(m3 - peak)
            inv_total = 1.0 / (near_weight * l0 + far_weight * l3)
            near_weight, far_weight = near_weight * inv_total, far_weight * inv_total
            out = near_weight * o0 + far_weight * o3
            kept.append((near_weight, far_weight, out))
            square = out * out if square is None else square + out * out
            cross = up * out if cross is None else cross + up * out
        for h, (near_weight, far_weight, out) in zip(hs, kept):
            f_near[h], f_s[3, h], attn[h] = near_weight, far_weight, out
        squares[...] += square
        crossed[...] += cross

    forward_group(3, {6 * R: global_bias}, (merge_load, merge), 4)
    rows8 = lax.broadcasted_iota(jnp.int32, (8, R), 0)
    squares_row = jnp.broadcast_to(jnp.sum(squares[...].T, 0, keepdims=True), (8, R))
    crossed_row = jnp.broadcast_to(jnp.sum(crossed[...].T, 0, keepdims=True), (8, R))
    st[...] = jnp.where(rows8 == 0, squares_row, crossed_row)
    stats = started(
        [
            remote(st, st_in.at[i], st_send.at[i], st_recv.at[i], peer)
            for i, peer in enumerate(head_peers)
        ]
    )

    def prepare(h, carry):
        q_t[h] = q_ref[:, head_cols(h)].T
        for g in range(3):
            f_s[g, h] = f_s[g, h] * f_near[h]
        factor, out = f_s[3, h], attn[h]
        up = ct_ref[:, head_cols(h)].astype(F32) * gains[pl.ds(h, 1)]
        up_sum = jnp.broadcast_to(jnp.sum(up * out, 1, keepdims=True), (R, HD))
        out_sum = jnp.broadcast_to(jnp.sum(out * out, 1, keepdims=True), (R, HD))
        up_sums[h], out_sums[h] = up_sum, out_sum
        e = expo[h, :, 6 * R :].astype(F32)
        x1 = (e * (nt((up * factor).astype(BF), vs[6 * R :]) - wide(up_sum * factor, G))).astype(BF)
        x2 = (e * (nt((out * factor).astype(BF), vs[6 * R :]) - wide(out_sum * factor, G))).astype(BF)
        xs[h, 0:R], xs[h, R : 2 * R] = x1, x2
        dqs[h] = nn(x1, ks[6 * R :])
        dq2[h] = nn(x2, ks[6 * R :])
        return carry

    lax.fori_loop(0, H, prepare, 0, unroll=2)
    dks[...] = jnp.zeros_like(dks)
    dvs[...] = jnp.zeros_like(dvs)
    waited(stats)
    both = st[...]
    for i in range(7):
        both = both + st_in[i]
    inverse_row = lax.rsqrt(both[0:1] / FEATURES + NORM_EPS)
    coef_row = inverse_row * inverse_row * inverse_row * both[1:2] / FEATURES
    inverse[...] = jnp.broadcast_to(inverse_row, (HD, R)).T
    coef[...] = jnp.broadcast_to(coef_row, (HD, R)).T

    inverse_t = jnp.broadcast_to(inverse_row, (HD, R))
    coef_t = jnp.broadcast_to(-coef_row, (HD, R))

    def global_grads(i, carry):
        kept = []
        for h in (4 * i, 4 * i + 1, 4 * i + 2, 4 * i + 3):
            out = attn[h]
            up = ct_ref[:, head_cols(h)].astype(F32) * gains[pl.ds(h, 1)]
            grad = inverse[...] * up - out * coef[...]
            slope = inverse[...] * up_sums[h] - coef[...] * out_sums[h]
            queries = q_t[h].astype(F32)
            both_t = jnp.concatenate([queries * inverse_t, queries * coef_t], 1).astype(BF)
            kept.append((h, grad, slope, both_t, (grad * f_s[3, h]).astype(BF).T))
        both_t = jnp.concatenate([k[3] for k in kept], 1)
        grad_t = jnp.concatenate([k[4] for k in kept], 1)
        x = xs[pl.ds(4 * i, 4)].reshape(8 * R, G)
        e = expo[pl.ds(4 * i, 4), :, 6 * R :].reshape(4 * R, G)
        d_keys, d_values = nn(both_t, x), nn(grad_t, e)
        dks[:, 6 * R :] += d_keys
        dvs[:, 6 * R :] += d_values
        for h, grad, slope, _, _ in kept:
            d_attn[h], diag[h] = grad, slope
        return carry

    def send_grads(b):
        lower = R * (b + 1)
        grad_out[b, 0] = (dks[:, lower : lower + R] * SCALE).astype(BF)
        grad_out[b, 1] = dvs[:, lower : lower + R].astype(BF)
        return started(
            [remote(grad_out.at[b], grad_in.at[b], gr_send.at[b], gr_recv.at[b], partners[b])]
        )

    lax.fori_loop(0, H // 4, global_grads, 0)
    d_global = jnp.concatenate([dks[:, 6 * R :] * SCALE, dvs[:, 6 * R :]], 0).astype(BF).T
    ga[1] = d_global.reshape(8, G // 8, 2 * HD)
    plane1 = started(plane_stage(1))
    backward_group(2, (5, 4), True)
    sent = send_grads(4) + send_grads(3)
    waited(plane1)
    add_plane(1)
    z1 = started(z_stage(1))
    backward_group(1, (3, 2))
    sent += send_grads(2) + send_grads(1)
    waited(z1)
    add_z(1)
    back1 = started(plane_back(1))
    backward_group(0, (1, 0))
    sent += send_grads(0)

    def finish(h, carry):
        dq_ref[:, head_cols(h)] = (dqs[h] * SCALE).astype(BF)
        normed_ref[:, head_cols(h)] = (attn[h] * inverse[...] * gains[pl.ds(h, 1)]).astype(BF)
        return carry

    lax.fori_loop(0, H, finish, 0)
    waited(sent)
    d_keys = dks[:, 0:R] * SCALE
    d_values = dvs[:, 0:R]
    for b in range(5):
        d_keys = d_keys + grad_in[b, 0].astype(F32)
        d_values = d_values + grad_in[b, 1].astype(F32)
    d_keys, d_values = d_keys.T, d_values.T
    waited(back1)
    back = nn(chosen, full[1].reshape(G, 2 * HD))
    dk_ref[...] = (d_keys + back[:, :HD]).astype(BF)
    dv_ref[...] = (d_values + back[:, HD:]).astype(BF)


def hand_over(*refs):
    sems = refs[8]
    copies = [pltpu.make_async_copy(refs[i], refs[4 + i], sems.at[i]) for i in range(4)]
    for copy in copies:
        copy.start()
    for copy in copies:
        copy.wait()


def per_device(queries, keys, values, key_keep, global_positions, gain, cotangent):
    vmem = pl.BlockSpec(memory_space=pltpu.VMEM)
    ng = len(GROUPS)
    eighth, width = G // 8, 2 * HD
    scratch = [
        pltpu.VMEM(queries.shape, BF),
        pltpu.VMEM(keys.shape, BF),
        pltpu.VMEM(values.shape, BF),
        pltpu.VMEM((1, R), jnp.int32),
        pltpu.VMEM((G // HD, HD), jnp.int32),
        pltpu.VMEM((H, HD), BF),
        pltpu.VMEM(cotangent.shape, BF),
        pltpu.SemaphoreType.DMA((7,)),
        pltpu.VMEM((SLOTS, HD), BF),
        pltpu.VMEM((SLOTS, HD), BF),
        pltpu.VMEM((5, 1, R), jnp.int32),
        pltpu.VMEM((R, R), F32),
        pltpu.VMEM((H, R, SLOTS), BF),
        *[pltpu.VMEM((ng, H, R, HD), F32)] * 4,
        *[pltpu.VMEM((H, R, HD), F32)] * 4,
        *[pltpu.VMEM((HD, SLOTS), F32)] * 2,
        pltpu.VMEM((2, 8, eighth, width), BF),
        pltpu.VMEM((2, 7, eighth, width), BF),
        pltpu.VMEM((2, eighth, width), BF),
        pltpu.VMEM((2, 3, eighth, width), BF),
        pltpu.VMEM((2, 8, eighth, width), BF),
        pltpu.VMEM((H, HD, R), BF),
        pltpu.VMEM((2, 1, G), F32),
        pltpu.VMEM((7, 1, G), F32),
        pltpu.VMEM((3, 1, G), F32),
        *[pltpu.VMEM((H, R, HD), F32)] * 2,
        pltpu.VMEM((H, 2 * R, G), BF),
        *[pltpu.VMEM((H, R, HD), F32)] * 2,
        pltpu.VMEM((H, HD), F32),
        *[pltpu.VMEM((R, HD), F32)] * 4,
        pltpu.VMEM((8, R), F32),
        pltpu.VMEM((7, 8, R), F32),
        pltpu.VMEM((5, 2, HD, R), BF),
        pltpu.VMEM((5, 2, HD, R), BF),
        pltpu.SemaphoreType.REGULAR,
        pltpu.SemaphoreType.REGULAR,
        *[pltpu.SemaphoreType.DMA((3, 5))] * 2,
        *[pltpu.SemaphoreType.DMA((2, 17))] * 2,
        *[pltpu.SemaphoreType.DMA((10,))] * 2,
        *[pltpu.SemaphoreType.DMA((7,))] * 2,
        *[pltpu.SemaphoreType.DMA((5,))] * 2,
    ]
    results = pl.pallas_call(
        kernel,
        out_shape=(
            jax.ShapeDtypeStruct(queries.shape, BF),
            jax.ShapeDtypeStruct(queries.shape, BF),
            jax.ShapeDtypeStruct(keys.shape, BF),
            jax.ShapeDtypeStruct(values.shape, BF),
        ),
        in_specs=[pl.BlockSpec(memory_space=pltpu.HBM)] * 7,
        out_specs=[vmem] * 4,
        scratch_shapes=scratch,
        compiler_params=pltpu.CompilerParams(
            collective_id=0, has_side_effects=True, vmem_limit_bytes=46 << 20
        ),
        name="butterfly",
    )(
        *[
            pltpu.with_memory_space_constraint(a, pltpu.HBM)
            for a in (
                queries,
                keys,
                values,
                key_keep.reshape(1, R),
                global_positions.reshape(G // HD, HD),
                gain.reshape(H, HD),
                cotangent,
            )
        ]
    )
    anywhere = pl.BlockSpec(memory_space=pl.ANY)
    return pl.pallas_call(
        hand_over,
        out_shape=tuple(jax.ShapeDtypeStruct(r.shape, r.dtype) for r in results),
        in_specs=[anywhere] * 4,
        out_specs=[anywhere] * 4,
        scratch_shapes=[pltpu.SemaphoreType.DMA((4,))],
        compiler_params=pltpu.CompilerParams(vmem_limit_bytes=1 << 20),
        name="hand_over",
    )(*results)


def solution(mesh):
    torus = Mesh(mesh.devices.reshape(4, 4, 2, 2, 4), (*SEQ, *HEAD))
    in_specs = (
        P(SEQ, HEAD), P(SEQ, HEAD), P(SEQ, HEAD), P(SEQ), P(), P(HEAD), P(SEQ, HEAD),
    )
    return jax.shard_map(
        per_device,
        mesh=torus,
        in_specs=in_specs,
        out_specs=(P(SEQ, HEAD),) * 4,
        check_vma=False,
    )
```

```python
import functools

import jax
import jax.numpy as jnp
from jax import lax
from jax.experimental import pallas as pl
from jax.experimental.pallas import tpu as pltpu
from jax.sharding import Mesh
from jax.sharding import PartitionSpec as P

HD = 128
FEATURES = 8192
NEG_FILL = -1e30
NORM_EPS = 1e-06
SEQ = ("x", "z", "c")
HEAD = ("zh", "y")
SCALE = HD ** (-0.5)
SCALE2 = SCALE * 1.4426950408889634
F32 = jnp.float32
BF = jnp.bfloat16
H = 8
R = 256
G = 384
SLOTS = 6 * R + G

BLOCKS = [(R * i, R) for i in range(6)] + [(6 * R, G)]
GROUPS = [(0, 1), (3, 2), (5, 4), (6,)]


def nt(a, b):
    return lax.dot_general(a, b, (((1,), (1,)), ((), ())), preferred_element_type=F32)


def nn(a, b):
    return jnp.dot(a, b, preferred_element_type=F32)


def tn(a, b):
    return lax.dot_general(a, b, (((0,), (0,)), ((), ())), preferred_element_type=F32)


def wide(x, n):
    return jnp.concatenate([x] * (n // 128), 1)


def head_cols(h):
    return pl.ds(pl.multiple_of(h * HD, HD), HD)


def kernel(
    q_hbm, k_hbm, v_hbm, keep_hbm, gpos_hbm, gain_hbm, ct_hbm,
    normed_ref, dq_ref, dk_ref, dv_ref,
    q_ref, k_ref, v_ref, keep_ref, gpos_ref, gain_ref, ct_ref, in_sems,
    ks, vs, keeps, own_bias, expo, m_s, l_s, o_s, f_s, attn, d_attn, diag, dqs, dks, dvs,
    ga, gx, pb, gz, full, q_t,
    fl, flx, flz,
    up_sums, out_sums, xs, dq2, f_near, gains, squares, crossed, inverse, coef, st, st_in, grad_out, grad_in,
    ring_sem, y_sem, kv_send, kv_recv, g_send, g_recv, f_send, f_recv, st_send, st_recv, gr_send, gr_recv,
):
    x, z, c = lax.axis_index("x"), lax.axis_index("z"), lax.axis_index("c")
    zh, y = lax.axis_index("zh"), lax.axis_index("y")
    plane_peers = [
        {"x": lax.rem(x + dx, 4), "c": c if dc == 0 else 1 - c}
        for dx in (2, 1, 3, 0)
        for dc in range(2)
        if dx or dc
    ]
    me = 2 * x + c
    z_peers = [lax.rem(z + o, 4) for o in (1, 2, 3)]
    head_peers = [
        {"zh": lax.rem(zh + dz, 2), "y": lax.rem(y + dy, 4)}
        for dz in range(2)
        for dy in range(4)
        if dz or dy
    ]
    partners = [
        {"c": 1 - c},
        {"z": z + 1 - 2 * lax.rem(z, 2)},
        {"z": lax.rem(z + 2, 4)},
        {"x": x + 1 - 2 * lax.rem(x, 2)},
        {"x": lax.rem(x + 2, 4)},
    ]

    def remote(src, dst, send, recv, device):
        return pltpu.make_async_remote_copy(
            src_ref=src, dst_ref=dst, send_sem=send, recv_sem=recv,
            device_id=device, device_id_type=pl.DeviceIdType.MESH,
        )

    barrier = pltpu.get_barrier_semaphore()
    at_end = 1 - lax.div(z * (3 - z), 2)
    across = {"zh": 1 - zh, "z": 3 - z}
    y_peers = [{"y": lax.rem(y + o, 4)} for o in (1, 2, 3)]
    y_near = [y_peers[0], y_peers[2]]
    near = plane_peers + [{"z": p} for p in z_peers] + y_near

    def signal_all(sem, peers):
        for peer in peers:
            pl.semaphore_signal(sem, inc=1, device_id=peer, device_id_type=pl.DeviceIdType.MESH)

    def signal_across(sem):
        @pl.when(at_end == 1)
        def _():
            signal_all(sem, [across])

    signal_all(barrier, near)
    signal_across(barrier)
    inputs = [
        pltpu.make_async_copy(src, dst, in_sems.at[i])
        for i, (src, dst) in enumerate(
            (
                (gpos_hbm, gpos_ref), (k_hbm, k_ref), (v_hbm, v_ref), (keep_hbm, keep_ref),
                (gain_hbm, gain_ref), (q_hbm, q_ref), (ct_hbm, ct_ref),
            )
        )
    ]
    for copy in inputs:
        copy.start()
    for copy in inputs[:4]:
        copy.wait()

    offset = (x * 8 + z * 2 + c) * R
    rows = lax.broadcasted_iota(jnp.int32, (R, G), 0)
    wanted = jnp.concatenate([jnp.broadcast_to(gpos_ref[j : j + 1], (R, HD)) for j in range(G // HD)], 1)
    chosen = (wanted - offset == rows).astype(F32).astype(BF)
    own_kv = jnp.concatenate([k_ref[...], v_ref[...]], 1)
    ga[0] = tn(chosen, own_kv).astype(BF).reshape(8, G // 8, 2 * HD)
    keep_rows = jnp.broadcast_to(keep_ref[...], (8, R)).astype(F32).astype(BF)
    fl[0] = nn(keep_rows, chosen)[0:1]
    eye = lax.broadcasted_iota(jnp.int32, (R, R), 0) == lax.broadcasted_iota(jnp.int32, (R, R), 1)
    row_bias = jnp.where(jnp.broadcast_to(keep_ref[...], (R, R)) == 1, 0.0, NEG_FILL)
    own_bias[...] = jnp.where(eye, 0.0, row_bias)
    ks[0:R] = k_ref[...]
    vs[0:R] = v_ref[...]

    pl.semaphore_wait(barrier, len(near) + at_end)
    signal_all(ring_sem, y_near)
    signal_across(ring_sem)

    def kv_copies(b):
        lower = R * (b + 1)
        return [
            remote(k_ref, ks.at[pl.ds(lower, R)], kv_send.at[0, b], kv_recv.at[0, b], partners[b]),
            remote(v_ref, vs.at[pl.ds(lower, R)], kv_send.at[1, b], kv_recv.at[1, b], partners[b]),
            remote(keep_ref, keeps.at[b], kv_send.at[2, b], kv_recv.at[2, b], partners[b]),
        ]

    def started(copies):
        for copy in copies:
            copy.start()
        return copies

    def waited(copies):
        for copy in copies:
            copy.wait()

    def plane_stage(t):
        return [
            remote(ga.at[t, 2 * p["x"] + p["c"]], gx.at[t, i], g_send.at[t, i], g_recv.at[t, i], p)
            for i, p in enumerate(plane_peers)
        ]

    def z_stage(t):
        return [
            remote(pb.at[t], gz.at[t, i], g_send.at[t, 7 + i], g_recv.at[t, 7 + i], {"z": p})
            for i, p in enumerate(z_peers)
        ]

    def plane_back(t):
        return [
            remote(full.at[t, me], full.at[t, me], g_send.at[t, 10 + i], g_recv.at[t, 10 + i], p)
            for i, p in enumerate(plane_peers)
        ]

    def add_plane(t):
        total = ga[t, me].astype(F32)
        for i in range(7):
            total = total + gx[t, i].astype(F32)
        pb[t] = total.astype(BF)

    def add_z(t):
        total = pb[t].astype(F32)
        for i in range(3):
            total = total + gz[t, i].astype(F32)
        full[t, me] = total.astype(BF)

    def flag_stage(s):
        peers = plane_peers if s == 0 else [{"z": p} for p in z_peers]
        into, base = (flx, 0) if s == 0 else (flz, 7)
        return [
            remote(fl.at[s], into.at[i], f_send.at[base + i], f_recv.at[base + i], p)
            for i, p in enumerate(peers)
        ]

    def forward_group(g, bias, after=None, heads=2):
        blocks = [BLOCKS[b] for b in GROUPS[g]]

        def body(i, carry):
            hs = [heads * i + j for j in range(heads)]
            queries = [q_ref[:, head_cols(h)] for h in hs]
            given = [after[0](h) for h in hs] if after is not None else None
            scores = []
            for q in queries:
                parts = []
                for lower, size in blocks:
                    s = nt(q, ks[lower : lower + size])
                    parts.append(s + (own_bias[...] if lower == 0 else bias[lower]))
                scores.append(parts)
            results = []
            for parts in scores:
                top = None
                for s in parts:
                    for j in range(0, s.shape[1], 128):
                        piece = s[:, j : j + 128]
                        top = piece if top is None else jnp.maximum(top, piece)
                peak = jnp.broadcast_to(jnp.max(top, 1, keepdims=True), (R, 128)) * SCALE2
                mixed, total, expos = None, None, []
                for (lower, size), s in zip(blocks, parts):
                    e = jnp.exp2(s * SCALE2 - wide(peak, size))
                    for j in range(0, size, 128):
                        piece = e[:, j : j + 128]
                        total = piece if total is None else total + piece
                    e_bf = e.astype(BF)
                    expos.append(e_bf)
                    term = nn(e_bf, vs[lower : lower + size])
                    mixed = term if mixed is None else mixed + term
                total = jnp.broadcast_to(jnp.sum(total, 1, keepdims=True), (R, 128))
                results.append((peak, total, mixed, expos))
            for h, (peak, total, mixed, expos) in zip(hs, results):
                for (lower, size), e_bf in zip(blocks, expos):
                    expo[h, :, lower : lower + size] = e_bf
                if after is None:
                    m_s[g, h], l_s[g, h], o_s[g, h] = peak, total, mixed
            if after is not None:
                after[1](hs, given, results)
            return carry

        lax.fori_loop(0, H // heads, body, 0)

    def backward_group(g, numbers, first=False):
        blocks = [BLOCKS[b] for b in numbers]

        def body(h, carry):
            factor = f_s[g, h]
            grad = (d_attn[h] * factor).astype(BF)
            shift = diag[h] * factor
            grad_t = grad.T
            d_query = None
            for lower, size in blocks:
                e = expo[h, :, lower : lower + size]
                d_probs = nt(grad, vs[lower : lower + size])
                d_scores = (e.astype(F32) * (d_probs - wide(shift, size))).astype(BF)
                term = nn(d_scores, ks[lower : lower + size])
                d_query = term if d_query is None else d_query + term
                dks[:, lower : lower + size] += nn(q_t[h], d_scores)
                dvs[:, lower : lower + size] += nn(grad_t, e)
            if first:
                dqs[h] = inverse[...] * dqs[h] - coef[...] * dq2[h] + d_query
            else:
                dqs[h] += d_query
            return carry

        lax.fori_loop(0, H, body, 0, unroll=2)

    def block_bias(*numbers):
        return {
            BLOCKS[b][0]: jnp.where(keeps[b - 1] == 1, 0.0, NEG_FILL).astype(F32) for b in numbers
        }

    plane0 = started(plane_stage(0) + flag_stage(0))
    kv = {b: started(kv_copies(b)) for b in (0, 2, 3, 1, 4)}
    for copy in inputs[4:]:
        copy.wait()
    gains[...] = gain_ref[...].astype(F32)
    waited(kv[0])
    forward_group(0, block_bias(1))
    pl.semaphore_wait(ring_sem, 2 + at_end)
    waited(plane0)
    add_plane(0)
    keep_plane = fl[0]
    for i in range(7):
        keep_plane = keep_plane + flx[i]
    fl[1] = keep_plane
    z0 = started(z_stage(0) + flag_stage(1))
    waited(kv[2])
    waited(kv[1])
    forward_group(1, block_bias(3, 2))
    waited(z0)
    signal_all(y_sem, y_peers)
    add_z(0)
    global_keep = fl[1] + flz[0] + flz[1] + flz[2]
    back0 = started(plane_back(0))
    waited(kv[3])
    waited(kv[4])
    forward_group(2, block_bias(5, 4))

    def merge_near(h, carry):
        peaks = [m_s[g, h] for g in range(3)]
        peak = functools.reduce(jnp.maximum, peaks)
        total, out = None, None
        for g, p in enumerate(peaks):
            weight = jnp.exp2(p - peak)
            f_s[g, h] = weight
            total = weight * l_s[g, h] if g == 0 else total + weight * l_s[g, h]
            out = weight * o_s[g, h] if g == 0 else out + weight * o_s[g, h]
        m_s[0, h], l_s[0, h], o_s[0, h] = peak, total, out
        return carry

    lax.fori_loop(0, H, merge_near, 0)
    waited(back0)
    lower = 6 * R
    all_kv = full[0].reshape(G, 2 * HD)
    ks[lower : lower + G] = all_kv[:, :HD]
    vs[lower : lower + G] = all_kv[:, HD:]
    global_bias = jnp.where(global_keep[0:1] > 0.5, 0.0, NEG_FILL)
    pl.semaphore_wait(y_sem, 3)
    squares[...] = jnp.zeros_like(squares)
    crossed[...] = jnp.zeros_like(crossed)

    def merge_load(h):
        up = ct_ref[:, head_cols(h)].astype(F32) * gains[pl.ds(h, 1)]
        return m_s[0, h], l_s[0, h], o_s[0, h], up

    def merge(hs, given, results):
        square, cross, kept = None, None, []
        for (m0, l0, o0, up), (m3, l3, o3, _) in zip(given, results):
            peak = jnp.maximum(m0, m3)
            near_weight, far_weight = jnp.exp2(m0 - peak), jnp.exp2(m3 - peak)
            inv_total = 1.0 / (near_weight * l0 + far_weight * l3)
            near_weight, far_weight = near_weight * inv_total, far_weight * inv_total
            out = near_weight * o0 + far_weight * o3
            kept.append((near_weight, far_weight, out))
            square = out * out if square is None else square + out * out
            cross = up * out if cross is None else cross + up * out
        for h, (near_weight, far_weight, out) in zip(hs, kept):
            f_near[h], f_s[3, h], attn[h] = near_weight, far_weight, out
        squares[...] += square
        crossed[...] += cross

    forward_group(3, {6 * R: global_bias}, (merge_load, merge), 4)
    rows8 = lax.broadcasted_iota(jnp.int32, (8, R), 0)
    squares_row = jnp.broadcast_to(jnp.sum(squares[...].T, 0, keepdims=True), (8, R))
    crossed_row = jnp.broadcast_to(jnp.sum(crossed[...].T, 0, keepdims=True), (8, R))
    st[...] = jnp.where(rows8 == 0, squares_row, crossed_row)
    stats = started(
        [
            remote(st, st_in.at[i], st_send.at[i], st_recv.at[i], peer)
            for i, peer in enumerate(head_peers)
        ]
    )

    def prepare(h, carry):
        q_t[h] = q_ref[:, head_cols(h)].T
        for g in range(3):
            f_s[g, h] = f_s[g, h] * f_near[h]
        factor, out = f_s[3, h], attn[h]
        up = ct_ref[:, head_cols(h)].astype(F32) * gains[pl.ds(h, 1)]
        up_sum = jnp.broadcast_to(jnp.sum(up * out, 1, keepdims=True), (R, HD))
        out_sum = jnp.broadcast_to(jnp.sum(out * out, 1, keepdims=True), (R, HD))
        up_sums[h], out_sums[h] = up_sum, out_sum
        e = expo[h, :, 6 * R :].astype(F32)
        x1 = (e * (nt((up * factor).astype(BF), vs[6 * R :]) - wide(up_sum * factor, G))).astype(BF)
        x2 = (e * (nt((out * factor).astype(BF), vs[6 * R :]) - wide(out_sum * factor, G))).astype(BF)
        xs[h, 0:R], xs[h, R : 2 * R] = x1, x2
        dqs[h] = nn(x1, ks[6 * R :])
        dq2[h] = nn(x2, ks[6 * R :])
        return carry

    lax.fori_loop(0, H, prepare, 0, unroll=2)
    dks[...] = jnp.zeros_like(dks)
    dvs[...] = jnp.zeros_like(dvs)
    waited(stats)
    both = st[...]
    for i in range(7):
        both = both + st_in[i]
    inverse_row = lax.rsqrt(both[0:1] / FEATURES + NORM_EPS)
    coef_row = inverse_row * inverse_row * inverse_row * both[1:2] / FEATURES
    inverse[...] = jnp.broadcast_to(inverse_row, (HD, R)).T
    coef[...] = jnp.broadcast_to(coef_row, (HD, R)).T

    inverse_t = jnp.broadcast_to(inverse_row, (HD, R))
    coef_t = jnp.broadcast_to(-coef_row, (HD, R))

    def global_grads(i, carry):
        kept = []
        for h in (4 * i, 4 * i + 1, 4 * i + 2, 4 * i + 3):
            out = attn[h]
            up = ct_ref[:, head_cols(h)].astype(F32) * gains[pl.ds(h, 1)]
            grad = inverse[...] * up - out * coef[...]
            slope = inverse[...] * up_sums[h] - coef[...] * out_sums[h]
            queries = q_t[h].astype(F32)
            both_t = jnp.concatenate([queries * inverse_t, queries * coef_t], 1).astype(BF)
            kept.append((h, grad, slope, both_t, (grad * f_s[3, h]).astype(BF).T))
        both_t = jnp.concatenate([k[3] for k in kept], 1)
        grad_t = jnp.concatenate([k[4] for k in kept], 1)
        x = xs[pl.ds(4 * i, 4)].reshape(8 * R, G)
        e = expo[pl.ds(4 * i, 4), :, 6 * R :].reshape(4 * R, G)
        d_keys, d_values = nn(both_t, x), nn(grad_t, e)
        dks[:, 6 * R :] += d_keys
        dvs[:, 6 * R :] += d_values
        for h, grad, slope, _, _ in kept:
            d_attn[h], diag[h] = grad, slope
        return carry

    def send_grads(b):
        lower = R * (b + 1)
        grad_out[b, 0] = (dks[:, lower : lower + R] * SCALE).astype(BF)
        grad_out[b, 1] = dvs[:, lower : lower + R].astype(BF)
        return started(
            [remote(grad_out.at[b], grad_in.at[b], gr_send.at[b], gr_recv.at[b], partners[b])]
        )

    lax.fori_loop(0, H // 4, global_grads, 0)
    d_global = jnp.concatenate([dks[:, 6 * R :] * SCALE, dvs[:, 6 * R :]], 0).astype(BF).T
    ga[1] = d_global.reshape(8, G // 8, 2 * HD)
    plane1 = started(plane_stage(1))
    backward_group(2, (5, 4), True)
    sent = send_grads(4) + send_grads(3)
    waited(plane1)
    add_plane(1)
    z1 = started(z_stage(1))
    backward_group(1, (3, 2))
    sent += send_grads(2) + send_grads(1)
    waited(z1)
    add_z(1)
    back1 = started(plane_back(1))
    backward_group(0, (1, 0))
    sent += send_grads(0)

    def finish(h, carry):
        dq_ref[:, head_cols(h)] = (dqs[h] * SCALE).astype(BF)
        normed_ref[:, head_cols(h)] = (attn[h] * inverse[...] * gains[pl.ds(h, 1)]).astype(BF)
        return carry

    lax.fori_loop(0, H, finish, 0)
    waited(sent)
    d_keys = dks[:, 0:R] * SCALE
    d_values = dvs[:, 0:R]
    for b in range(5):
        d_keys = d_keys + grad_in[b, 0].astype(F32)
        d_values = d_values + grad_in[b, 1].astype(F32)
    d_keys, d_values = d_keys.T, d_values.T
    waited(back1)
    back = nn(chosen, full[1].reshape(G, 2 * HD))
    dk_ref[...] = (d_keys + back[:, :HD]).astype(BF)
    dv_ref[...] = (d_values + back[:, HD:]).astype(BF)


def hand_over(*refs):
    sems = refs[8]
    copies = [pltpu.make_async_copy(refs[i], refs[4 + i], sems.at[i]) for i in range(4)]
    for copy in copies:
        copy.start()
    for copy in copies:
        copy.wait()


def per_device(queries, keys, values, key_keep, global_positions, gain, cotangent):
    vmem = pl.BlockSpec(memory_space=pltpu.VMEM)
    ng = len(GROUPS)
    eighth, width = G // 8, 2 * HD
    scratch = [
        pltpu.VMEM(queries.shape, BF),
        pltpu.VMEM(keys.shape, BF),
        pltpu.VMEM(values.shape, BF),
        pltpu.VMEM((1, R), jnp.int32),
        pltpu.VMEM((G // HD, HD), jnp.int32),
        pltpu.VMEM((H, HD), BF),
        pltpu.VMEM(cotangent.shape, BF),
        pltpu.SemaphoreType.DMA((7,)),
        pltpu.VMEM((SLOTS, HD), BF),
        pltpu.VMEM((SLOTS, HD), BF),
        pltpu.VMEM((5, 1, R), jnp.int32),
        pltpu.VMEM((R, R), F32),
        pltpu.VMEM((H, R, SLOTS), BF),
        *[pltpu.VMEM((ng, H, R, HD), F32)] * 4,
        *[pltpu.VMEM((H, R, HD), F32)] * 4,
        *[pltpu.VMEM((HD, SLOTS), F32)] * 2,
        pltpu.VMEM((2, 8, eighth, width), BF),
        pltpu.VMEM((2, 7, eighth, width), BF),
        pltpu.VMEM((2, eighth, width), BF),
        pltpu.VMEM((2, 3, eighth, width), BF),
        pltpu.VMEM((2, 8, eighth, width), BF),
        pltpu.VMEM((H, HD, R), BF),
        pltpu.VMEM((2, 1, G), F32),
        pltpu.VMEM((7, 1, G), F32),
        pltpu.VMEM((3, 1, G), F32),
        *[pltpu.VMEM((H, R, HD), F32)] * 2,
        pltpu.VMEM((H, 2 * R, G), BF),
        *[pltpu.VMEM((H, R, HD), F32)] * 2,
        pltpu.VMEM((H, HD), F32),
        *[pltpu.VMEM((R, HD), F32)] * 4,
        pltpu.VMEM((8, R), F32),
        pltpu.VMEM((7, 8, R), F32),
        pltpu.VMEM((5, 2, HD, R), BF),
        pltpu.VMEM((5, 2, HD, R), BF),
        pltpu.SemaphoreType.REGULAR,
        pltpu.SemaphoreType.REGULAR,
        *[pltpu.SemaphoreType.DMA((3, 5))] * 2,
        *[pltpu.SemaphoreType.DMA((2, 17))] * 2,
        *[pltpu.SemaphoreType.DMA((10,))] * 2,
        *[pltpu.SemaphoreType.DMA((7,))] * 2,
        *[pltpu.SemaphoreType.DMA((5,))] * 2,
    ]
    results = pl.pallas_call(
        kernel,
        out_shape=(
            jax.ShapeDtypeStruct(queries.shape, BF),
            jax.ShapeDtypeStruct(queries.shape, BF),
            jax.ShapeDtypeStruct(keys.shape, BF),
            jax.ShapeDtypeStruct(values.shape, BF),
        ),
        in_specs=[pl.BlockSpec(memory_space=pltpu.HBM)] * 7,
        out_specs=[vmem] * 4,
        scratch_shapes=scratch,
        compiler_params=pltpu.CompilerParams(
            collective_id=0, has_side_effects=True, vmem_limit_bytes=46 << 20
        ),
        name="butterfly",
    )(
        *[
            pltpu.with_memory_space_constraint(a, pltpu.HBM)
            for a in (
                queries,
                keys,
                values,
                key_keep.reshape(1, R),
                global_positions.reshape(G // HD, HD),
                gain.reshape(H, HD),
                cotangent,
            )
        ]
    )
    anywhere = pl.BlockSpec(memory_space=pl.ANY)
    return pl.pallas_call(
        hand_over,
        out_shape=tuple(jax.ShapeDtypeStruct(r.shape, r.dtype) for r in results),
        in_specs=[anywhere] * 4,
        out_specs=[anywhere] * 4,
        scratch_shapes=[pltpu.SemaphoreType.DMA((4,))],
        compiler_params=pltpu.CompilerParams(vmem_limit_bytes=1 << 20),
        name="hand_over",
    )(*results)


def solution(mesh):
    torus = Mesh(mesh.devices.reshape(4, 4, 2, 2, 4), (*SEQ, *HEAD))
    in_specs = (
        P(SEQ, HEAD), P(SEQ, HEAD), P(SEQ, HEAD), P(SEQ), P(), P(HEAD), P(SEQ, HEAD),
    )
    return jax.shard_map(
        per_device,
        mesh=torus,
        in_specs=in_specs,
        out_specs=(P(SEQ, HEAD),) * 4,
        check_vma=False,
    )
```
